256 devices in a mesh: row: 4 (over y_hi, core), col: 32 (over z, x), layer: 2 (over y_lo).
Axes of the slice: x: 4, y: 4 (y_hi: 2, y_lo: 2; y = y_hi * 2 + y_lo), z: 8, core: 2. Of those that a mesh axis runs over, the one named last changes fastest.
Arguments:
- density: bfloat16 [4096, 4096], P('row', 'col'), may hold values from -0.44921875 to 0.44921875
- pattern: int32 [32, 32], replicated, may hold values from 0 to 1, as said below
Outputs:
- purified: float32 [4096, 4096], P(('row', 'layer'), 'col')
The draws below stay inside these ranges and needn't reach their ends.
Inputs may be any that keep to these rules, and one draw needn't show every extreme that they name: `pattern`: every diagonal block is kept.
All inputs are finite; a program needn't handle non-finite values.
Results may differ from the reference program's by a relative error of at most 0.00071.
Values may be sent and summed in bfloat16 or wider, within the bound.
No kernel may reach another device: no remote copies, remote signals or barrier semaphores. Data moves between devices by JAX's collectives and lax.ppermute only.
A program may use at most 64 MiB of HBM per device.

```python
import jax
import jax.numpy as jnp

BLOCK = 128
ORDER = 4096
NBLK = 32


def draw_pattern(key, part):
    random_bits = jax.random.randint(jax.random.fold_in(key, 17), (NBLK, NBLK), 0, 2).astype(jnp.int32)
    indices = jnp.arange(NBLK, dtype=jnp.int32)
    diagonal = indices[:, None] == indices[None, :]
    return jnp.where(diagonal, jnp.ones_like(random_bits), random_bits).astype(jnp.int32)


def steps_of(rng, extent, shards, least, top_value):
    factor_of = 1.0
    for dim, parts in shards:
        steps = jax.random.uniform(jax.random.fold_in(jax.random.fold_in(rng, 6), dim), (parts,), jnp.float32, least / len(shards), top_value / len(shards))
        factor_of = factor_of * jnp.repeat(jnp.exp(steps), extent[dim] // parts).reshape((-1,) + (1,) * (len(extent) - 1 - dim))
    return factor_of


def scatter_about(stream_key, extent, deviation, most, cuts=(), kind=jnp.bfloat16):
    entries = deviation * jax.random.normal(stream_key, extent, jnp.float32)
    if cuts:
        entries = entries * steps_of(stream_key, extent, cuts, -0.22, 0.18)
    return jnp.clip(entries, -most, most).astype(kind)


def setup_inputs(seed: int = 0) -> dict:
    splits = jax.random.split(jax.random.key(seed), 3)
    density = scatter_about(splits[0], (ORDER, ORDER), 0.074, 0.44921875, ((0, 4), (1, 32)))
    pattern = draw_pattern(jax.random.fold_in(splits[2], 71), 0)
    return dict(density=density, pattern=pattern)


def reference(density, pattern):
    full_mask = jnp.repeat(jnp.repeat(pattern, BLOCK, axis=0), BLOCK, axis=1)
    sparse = jnp.where(full_mask == 1, density, jnp.zeros_like(density)).astype(jnp.bfloat16)
    square = jnp.dot(sparse, sparse, preferred_element_type=jnp.float32)
    square_half = square.astype(jnp.bfloat16)
    cube = jnp.dot(square_half, sparse, preferred_element_type=jnp.float32)
    return 3.0 * square - 2.0 * cube
```

```python
import functools

import jax
import jax.numpy as jnp
from jax import lax
from jax.experimental import pallas as pl
from jax.experimental.pallas import tpu as pltpu
from jax.sharding import Mesh, PartitionSpec as P


AXES = ("yh", "core", "z", "x", "yl")
NX, NZ = 4, 8
BLK = 128
VMEM = pl.BlockSpec(memory_space=pltpu.VMEM)
SMEM = pl.BlockSpec(memory_space=pltpu.SMEM)
bf16, f32 = jnp.bfloat16, jnp.float32


def call(kernel, outs, ins, flops=0, nbytes=0):
    return pl.pallas_call(
        kernel,
        out_shape=outs,
        in_specs=ins,
        out_specs=jax.tree.map(lambda _: VMEM, outs),
        cost_estimate=pl.CostEstimate(flops=flops, bytes_accessed=nbytes, transcendentals=0),
    )


def to_x(a, k):
    return lax.ppermute(a, "x", [(i, (i + k) % NX) for i in range(NX)])


def to_z(a, k):
    return lax.ppermute(a, "z", [(i, (i + k) % NZ) for i in range(NZ)])


def to_core(a):
    return lax.ppermute(a, "core", [(0, 1), (1, 0)])


def cross(a, k):
    pairs = []
    for yh in range(2):
        for x in range(NX):
            for yl in range(2):
                src = (yh * NX + x) * 2 + yl
                dst = ((1 - yh) * NX + (x + k) % NX) * 2 + (1 - yl)
                pairs.append((src, dst))
    return lax.ppermute(a, ("yh", "x", "yl"), pairs)


def rows_at(i):
    return pl.ds(pl.multiple_of(i * BLK, BLK), BLK)


def mask_kernel(pattern, density, sparse, *pieces):
    first = (lax.axis_index("yh") * 2 + lax.axis_index("core")) * 8
    column = lax.axis_index("z") * NX + lax.axis_index("x")
    for i in range(8):
        rows = slice(i * BLK, (i + 1) * BLK)
        keep = pattern[first + i, column] == 1
        block = density[rows, :]
        sparse[rows, :] = jnp.where(keep, block, jnp.zeros_like(block))
    x, yl = lax.axis_index("x"), lax.axis_index("yl")
    for k, piece in enumerate(pieces):
        piece[...] = sparse[rows_at(yl * 4 + lax.rem(x + k, NX)), :]


def shard_kernel(*refs):
    *pieces, shard = refs
    x = lax.axis_index("x")
    for k, piece in enumerate(pieces):
        shard[:, rows_at(lax.rem(x - k + NX, NX))] = piece[...]


def panel_kernel(*refs):
    *blocks, panel = refs
    x = lax.axis_index("x")
    yh, core = lax.axis_index("yh"), lax.axis_index("core")
    for n, block in enumerate(blocks):
        k, dyh, dcore = n % 4, n // 4 % 2, n // 8
        group = lax.rem(yh + dyh, 2) * 2 + lax.rem(core + dcore, 2)
        panel[pl.ds(pl.multiple_of(group * 1024, 1024), 1024), rows_at(lax.rem(x - k + NX, NX))] = block[...]


SHIFTS = (0, 1, -1, 2, -2, 3, -3)


def product(shards, low, high, panel):
    z = lax.axis_index("z")
    total = None

    def part(lhs, k):
        owner = lax.rem(z - k + NZ, NZ)
        rhs = panel[pl.ds(pl.multiple_of(owner * 512, 512), 512), :]
        return jnp.dot(lhs, rhs, preferred_element_type=f32)

    for k, shard in zip(SHIFTS, shards):
        term = part(shard[...], k)
        total = term if total is None else total + term
    far = jnp.concatenate([low[...], high[...]], axis=0)
    return total + part(far, 4)


def square_kernel(*refs):
    *shards, low, high, panel, square, half = refs
    value = product(shards, low, high, panel)
    square[...] = value
    half[...] = value.astype(bf16)


def cube_kernel(*refs):
    *shards, low, high, panel, square = refs[:11]
    pieces = refs[11:15]
    total = refs[15]
    total[...] = 3.0 * square[...] - 2.0 * product(shards, low, high, panel)
    x = lax.axis_index("x")
    for k, piece in enumerate(pieces):
        piece[...] = total[:, rows_at(lax.rem(x + k, NX))]


def join_kernel(*refs):
    *pieces, out = refs
    x = lax.axis_index("x")
    for k, piece in enumerate(pieces):
        out[rows_at(lax.rem(x - k + NX, NX)), :] = piece[...]


def gather_z(a):
    got = {0: a}
    for k in (2, -2, 1, -1):
        got[k] = to_z(a, k)
    got[3], got[-3] = to_z(got[2], 1), to_z(got[-2], -1)
    low, high = to_z(got[2][:64], 2), to_z(got[-2][64:], -2)
    return [got[k] for k in SHIFTS] + [low, high]


def shape(rows, cols, dtype):
    return jax.ShapeDtypeStruct((rows, cols), dtype)


def body(density, pattern):
    piece = shape(BLK, BLK, bf16)
    sparse, *pieces = call(mask_kernel, [shape(1024, BLK, bf16)] + [piece] * 4, [SMEM, VMEM])(pattern, density)
    pieces = [pieces[0]] + [to_x(pieces[k], k) for k in (1, 2, 3)]
    shard = call(shard_kernel, shape(BLK, 512, bf16), [VMEM] * 4)(*pieces)
    lefts = gather_z(shard)

    blocks = [sparse] + [to_x(sparse, k) for k in (1, 2, 3)] + [cross(sparse, k) for k in (0, 1, 2, 3)]
    blocks = blocks + [to_core(b) for b in blocks]
    panel = call(panel_kernel, shape(4096, 512, bf16), [VMEM] * 16, nbytes=8 << 20)(*blocks)

    flops = 2 * 128 * 4096 * 512
    square, half = call(square_kernel, [shape(BLK, 512, f32), shape(BLK, 512, bf16)], [VMEM] * 10, flops, 5 << 20)(*lefts, panel)
    lefts = gather_z(half)
    pieces = pl.pallas_call(
        cube_kernel,
        out_shape=[shape(BLK, BLK, f32)] * 4,
        in_specs=[VMEM] * 11,
        out_specs=[VMEM] * 4,
        scratch_shapes=[pltpu.VMEM((BLK, 512), f32)],
        cost_estimate=pl.CostEstimate(flops=flops, bytes_accessed=5 << 20, transcendentals=0),
    )(*lefts, panel, square)
    pieces = [pieces[0]] + [to_x(pieces[k], k) for k in (1, 2, 3)]
    return call(join_kernel, shape(512, BLK, f32), [VMEM] * 4)(*pieces)


def solution(mesh):
    fine = Mesh(mesh.devices.reshape(2, 2, NZ, NX, 2), AXES)
    return jax.shard_map(
        body,
        mesh=fine,
        in_specs=(P(("yh", "core"), ("z", "x")), P()),
        out_specs=P(("yh", "core", "yl"), ("z", "x")),
        check_vma=False,
    )
```

```python
import jax
import jax.numpy as jnp
from jax import lax
from jax.experimental import pallas as pl
from jax.experimental.pallas import tpu as pltpu
from jax.sharding import Mesh, PartitionSpec as P


AXES = ("yh", "core", "z", "x", "yl")
NX, NZ = 4, 8
BLK = 128
VMEM = pl.BlockSpec(memory_space=pltpu.VMEM)
SMEM = pl.BlockSpec(memory_space=pltpu.SMEM)
bf16, f32 = jnp.bfloat16, jnp.float32
PARAMS = pltpu.CompilerParams(vmem_limit_bytes=16 << 20)


def call(kernel, outs, ins, flops=0, nbytes=0, scratch=()):
    return pl.pallas_call(
        kernel,
        out_shape=outs,
        in_specs=ins,
        out_specs=jax.tree.map(lambda _: VMEM, outs),
        scratch_shapes=scratch,
        compiler_params=PARAMS,
        cost_estimate=pl.CostEstimate(flops=flops, bytes_accessed=nbytes, transcendentals=0),
    )


def shape(rows, cols, dtype):
    return jax.ShapeDtypeStruct((rows, cols), dtype)


def to_x(a, k):
    return lax.ppermute(a, "x", [(i, (i + k) % NX) for i in range(NX)])


def along_z(a, k):
    pairs = [(z, (z + k) % NZ) for z in range(NZ)] + [(NZ + z, NZ + (z - k) % NZ) for z in range(NZ)]
    return lax.ppermute(a, ("core", "z"), pairs)


def to_core(a):
    return lax.ppermute(a, "core", [(0, 1), (1, 0)])


def cross(a, k):
    pairs = []
    for yh in range(2):
        for x in range(NX):
            for yl in range(2):
                src = (yh * NX + x) * 2 + yl
                dst = ((1 - yh) * NX + (x + k) % NX) * 2 + (1 - yl)
                pairs.append((src, dst))
    return lax.ppermute(a, ("yh", "x", "yl"), pairs)


def at(i, size=BLK):
    return pl.ds(pl.multiple_of(i * size, size), size)


def back(i, k, n):
    return lax.rem(i - k + n, n)


def kept(pattern, row, column, block):
    return jnp.where(pattern[row, column] == 1, block, jnp.zeros_like(block))


def pieces_kernel(density, *pieces):
    x, yl = lax.axis_index("x"), lax.axis_index("yl")
    for k, piece in enumerate(pieces):
        piece[...] = density[at(yl * 4 + lax.rem(x + k, NX)), :]


def shard_kernel(pattern, *refs):
    *pieces, shard = refs
    x, z = lax.axis_index("x"), lax.axis_index("z")
    row = (lax.axis_index("yh") * 2 + lax.axis_index("core")) * 8 + lax.axis_index("yl") * 4 + x
    for k, piece in enumerate(pieces):
        source = back(x, k, NX)
        shard[:, at(source)] = kept(pattern, row, z * NX + source, piece[...])


def panel_kernel(pattern, *refs):
    *blocks, panel = refs
    x, z = lax.axis_index("x"), lax.axis_index("z")
    yh, core = lax.axis_index("yh"), lax.axis_index("core")
    for n, block in enumerate(blocks):
        k, dyh, dcore = n % 4, n // 4 % 2, n // 8
        group = lax.rem(yh + dyh, 2) * 2 + lax.rem(core + dcore, 2)
        source = back(x, k, NX)
        for i in range(8):
            part = block[i * BLK : (i + 1) * BLK, :]
            panel[at(group * 8 + i), at(source)] = kept(pattern, group * 8 + i, z * NX + source, part)


def join_cores_kernel(mine, other, both):
    core = lax.axis_index("core")
    both[at(core), :] = mine[...]
    both[at(1 - core), :] = other[...]


def split_kernel(both, *parts):
    core = lax.axis_index("core")
    parts[0][...] = both[at(1 - core), :]
    if len(parts) > 1:
        parts[1][...] = both[at(core), :]


def product(refs, panel):
    own, near2, near1, near3, far, back2, back1, back3 = refs
    core, z = lax.axis_index("core"), lax.axis_index("z")
    sign = 1 - 2 * core

    def part(lhs, k):
        owner = lax.rem(z - sign * k + NZ, NZ)
        return jnp.dot(lhs, panel[at(owner, 512), :], preferred_element_type=f32)

    total = part(own[...], 0)
    for k, ref in ((1, near1), (2, near2), (3, near3)):
        total += part(ref[at(core), :], k)
    for k, ref in ((-1, back1), (-2, back2), (-3, back3), (4, far)):
        total += part(ref[...], k)
    return total


def square_kernel(*refs):
    *lefts, panel, square, half = refs
    value = product(lefts, panel)
    square[...] = value
    half[...] = value.astype(bf16)


def cube_kernel(*refs):
    lefts, (panel, square), pieces, total = refs[:8], refs[8:10], refs[10:14], refs[14]
    total[...] = 3.0 * square[...] - 2.0 * product(lefts, panel)
    x = lax.axis_index("x")
    for k, piece in enumerate(pieces):
        piece[...] = total[:, at(lax.rem(x + k, NX))]


def join_kernel(*refs):
    *pieces, out = refs
    x = lax.axis_index("x")
    for k, piece in enumerate(pieces):
        out[at(back(x, k, NX)), :] = piece[...]


def gather_z(own):
    part = shape(BLK, 512, bf16)
    other = to_core(own)
    both = call(join_cores_kernel, shape(2 * BLK, 512, bf16), [VMEM] * 2)(own, other)
    near2 = along_z(both, 2)
    near1 = along_z(both, 1)
    near3 = along_z(near2, 1)
    send2, relay = call(split_kernel, [part] * 2, [VMEM])(near2)
    far = along_z(relay, 2)
    back2 = to_core(send2)
    back1 = to_core(call(split_kernel, [part], [VMEM])(near1)[0])
    back3 = to_core(call(split_kernel, [part], [VMEM])(near3)[0])
    return [own, near2, near1, near3, far, back2, back1, back3]


def step(density, pattern):
    piece = shape(BLK, BLK, bf16)
    pieces = call(pieces_kernel, [piece] * 4, [VMEM])(density)
    pieces = [pieces[0]] + [to_x(pieces[k], k) for k in (1, 2, 3)]
    shard = call(shard_kernel, shape(BLK, 512, bf16), [SMEM] + [VMEM] * 4)(pattern, *pieces)
    lefts = gather_z(shard)

    blocks = [density] + [to_x(density, k) for k in (1, 2, 3)]
    blocks = blocks + [cross(density, k) for k in (0, 1, 2, 3)]
    blocks = blocks + [to_core(b) for b in blocks]
    panel = call(panel_kernel, shape(4096, 512, bf16), [SMEM] + [VMEM] * 16, nbytes=8 << 20)(pattern, *blocks)

    flops = 2 * 128 * 4096 * 512
    square, half = call(square_kernel, [shape(BLK, 512, f32), shape(BLK, 512, bf16)], [VMEM] * 9, flops, 5 << 20)(*lefts, panel)
    lefts = gather_z(half)
    pieces = call(cube_kernel, [shape(BLK, BLK, f32)] * 4, [VMEM] * 10, flops, 5 << 20, [pltpu.VMEM((BLK, 512), f32)])(*lefts, panel, square)
    pieces = [pieces[0]] + [to_x(pieces[k], k) for k in (1, 2, 3)]
    return call(join_kernel, shape(512, BLK, f32), [VMEM] * 4)(*pieces)


def solution(mesh):
    fine = Mesh(mesh.devices.reshape(2, 2, NZ, NX, 2), AXES)
    return jax.shard_map(
        step,
        mesh=fine,
        in_specs=(P(("yh", "core"), ("z", "x")), P()),
        out_specs=P(("yh", "core", "yl"), ("z", "x")),
        check_vma=False,
    )
```

```python
import jax
import jax.numpy as jnp
from jax import lax
from jax.experimental import pallas as pl
from jax.experimental.pallas import tpu as pltpu
from jax.sharding import Mesh, PartitionSpec as P


AXES = ("yh", "core", "z", "x", "yl")
NX, NZ = 4, 8
BLK = 128
VMEM = pl.BlockSpec(memory_space=pltpu.VMEM)
HBM = pl.BlockSpec(memory_space=pltpu.HBM)
bf16, f32 = jnp.bfloat16, jnp.float32
PARAMS = pltpu.CompilerParams(vmem_limit_bytes=16 << 20)


def call(kernel, outs, ins, flops=0, nbytes=0, scratch=()):
    return pl.pallas_call(
        kernel,
        out_shape=outs,
        in_specs=ins,
        out_specs=jax.tree.map(lambda _: VMEM, outs),
        scratch_shapes=scratch,
        compiler_params=PARAMS,
        cost_estimate=pl.CostEstimate(flops=flops, bytes_accessed=nbytes, transcendentals=0),
    )


def shape(rows, cols, dtype):
    return jax.ShapeDtypeStruct((rows, cols), dtype)


def to_x(a, k):
    return lax.ppermute(a, "x", [(i, (i + k) % NX) for i in range(NX)])


def along_z(a, k):
    pairs = [(z, (z + k) % NZ) for z in range(NZ)] + [(NZ + z, NZ + (z - k) % NZ) for z in range(NZ)]
    return lax.ppermute(a, ("core", "z"), pairs)


def to_core(a):
    return lax.ppermute(a, "core", [(0, 1), (1, 0)])


def cross(a):
    return lax.ppermute(a, ("yh", "yl"), [(0, 3), (3, 0), (1, 2), (2, 1)])


def at(i, size=BLK):
    return pl.ds(pl.multiple_of(i * size, size), size)


def back(i, k, n):
    return lax.rem(i - k + n, n)


def mask_kernel(pattern, density, sparse, *rest):
    *pieces, flags, block, sems = rest
    copies = [
        pltpu.make_async_copy(pattern, flags, sems.at[0]),
        pltpu.make_async_copy(density, block, sems.at[1]),
    ]
    for copy in copies:
        copy.start()
    for copy in copies:
        copy.wait()
    first = (lax.axis_index("yh") * 2 + lax.axis_index("core")) * 8
    column = lax.axis_index("z") * NX + lax.axis_index("x")
    for i in range(8):
        rows = slice(i * BLK, (i + 1) * BLK)
        value = block[rows, :]
        sparse[rows, :] = jnp.where(flags[first + i, column] == 1, value, jnp.zeros_like(value))
    x, yl = lax.axis_index("x"), lax.axis_index("yl")
    for k, piece in enumerate(pieces):
        piece[...] = sparse[at(yl * 4 + lax.rem(x + k, NX)), :]


def shard_kernel(*refs):
    *pieces, shard = refs
    x = lax.axis_index("x")
    for k, piece in enumerate(pieces):
        shard[:, at(back(x, k, NX))] = piece[...]


def panel_kernel(*refs):
    *blocks, panel = refs
    x = lax.axis_index("x")
    yh, core = lax.axis_index("yh"), lax.axis_index("core")
    for n, block in enumerate(blocks):
        k, dyh, dcore = n % 4, n // 4 % 2, n // 8
        group = lax.rem(yh + dyh, 2) * 2 + lax.rem(core + dcore, 2)
        panel[at(group, 1024), at(back(x, k, NX))] = block[...]


def join_cores_kernel(mine, other, both):
    core = lax.axis_index("core")
    both[at(core), :] = mine[...]
    both[at(1 - core), :] = other[...]


def split_kernel(both, *parts):
    core = lax.axis_index("core")
    parts[0][...] = both[at(1 - core), :]
    if len(parts) > 1:
        parts[1][...] = both[at(core), :]


def product(refs, panel):
    own, near2, near1, near3, far, back2, back1, back3 = refs
    core, z = lax.axis_index("core"), lax.axis_index("z")
    sign = 1 - 2 * core

    def part(lhs, k):
        owner = lax.rem(z - sign * k + NZ, NZ)
        return jnp.dot(lhs, panel[at(owner, 512), :], preferred_element_type=f32)

    total = part(own[...], 0)
    for k, ref in ((1, near1), (2, near2), (3, near3)):
        total += part(ref[at(core), :], k)
    for k, ref in ((-1, back1), (-2, back2), (-3, back3), (4, far)):
        total += part(ref[...], k)
    return total


def square_kernel(*refs):
    *lefts, panel, square, half = refs
    value = product(lefts, panel)
    square[...] = value
    half[...] = value.astype(bf16)


def cube_kernel(*refs):
    lefts, (panel, square), pieces, total = refs[:8], refs[8:10], refs[10:14], refs[14]
    total[...] = 3.0 * square[...] - 2.0 * product(lefts, panel)
    x = lax.axis_index("x")
    for k, piece in enumerate(pieces):
        piece[...] = total[:, at(lax.rem(x + k, NX))]


def join_kernel(*refs):
    *pieces, out = refs
    x = lax.axis_index("x")
    for k, piece in enumerate(pieces):
        out[at(back(x, k, NX)), :] = piece[...]


def gather_z(own):
    part = shape(BLK, 512, bf16)
    other = to_core(own)
    both = call(join_cores_kernel, shape(2 * BLK, 512, bf16), [VMEM] * 2)(own, other)
    near2 = along_z(both, 2)
    near1 = along_z(both, 1)
    near3 = along_z(near2, 1)
    send2, relay = call(split_kernel, [part] * 2, [VMEM])(near2)
    far = along_z(relay, 2)
    back2 = to_core(send2)
    back1 = to_core(call(split_kernel, [part], [VMEM])(near1)[0])
    back3 = to_core(call(split_kernel, [part], [VMEM])(near3)[0])
    return [own, near2, near1, near3, far, back2, back1, back3]


def step(density, pattern):
    piece = shape(BLK, BLK, bf16)
    own = [pltpu.SMEM((32, 32), jnp.int32), pltpu.VMEM((1024, BLK), bf16), pltpu.SemaphoreType.DMA((2,))]
    sparse, *pieces = call(mask_kernel, [shape(1024, BLK, bf16)] + [piece] * 4, [HBM] * 2, scratch=own)(pattern, density)
    pieces = [pieces[0]] + [to_x(pieces[k], k) for k in (1, 2, 3)]
    shard = call(shard_kernel, shape(BLK, 512, bf16), [VMEM] * 4)(*pieces)
    lefts = gather_z(shard)

    crossed = cross(sparse)
    blocks = [sparse] + [to_x(sparse, k) for k in (1, 2, 3)]
    blocks = blocks + [crossed] + [to_x(crossed, k) for k in (1, 2, 3)]
    blocks = blocks + [to_core(b) for b in blocks]
    panel = call(panel_kernel, shape(4096, 512, bf16), [VMEM] * 16, nbytes=8 << 20)(*blocks)

    flops = 2 * 128 * 4096 * 512
    square, half = call(square_kernel, [shape(BLK, 512, f32), shape(BLK, 512, bf16)], [VMEM] * 9, flops, 5 << 20)(*lefts, panel)
    lefts = gather_z(half)
    pieces = call(cube_kernel, [shape(BLK, BLK, f32)] * 4, [VMEM] * 10, flops, 5 << 20, [pltpu.VMEM((BLK, 512), f32)])(*lefts, panel, square)
    pieces = [pieces[0]] + [to_x(pieces[k], k) for k in (1, 2, 3)]
    return call(join_kernel, shape(512, BLK, f32), [VMEM] * 4)(*pieces)


def solution(mesh):
    fine = Mesh(mesh.devices.reshape(2, 2, NZ, NX, 2), AXES)
    return jax.shard_map(
        step,
        mesh=fine,
        in_specs=(P(("yh", "core"), ("z", "x")), P()),
        out_specs=P(("yh", "core", "yl"), ("z", "x")),
        check_vma=False,
    )
```

```python
import jax
import jax.numpy as jnp
from jax import lax
from jax.experimental import pallas as pl
from jax.experimental.pallas import tpu as pltpu
from jax.sharding import Mesh, PartitionSpec as P


AXES = ("yh", "core", "z", "x", "yl")
NX, NZ = 4, 8
BLK = 128
VMEM = pl.BlockSpec(memory_space=pltpu.VMEM)
HBM = pl.BlockSpec(memory_space=pltpu.HBM)
bf16, f32 = jnp.bfloat16, jnp.float32
PARAMS = pltpu.CompilerParams(vmem_limit_bytes=16 << 20)


def call(kernel, outs, ins, flops=0, nbytes=0, scratch=()):
    return pl.pallas_call(
        kernel,
        out_shape=outs,
        in_specs=ins,
        out_specs=jax.tree.map(lambda _: VMEM, outs),
        scratch_shapes=scratch,
        compiler_params=PARAMS,
        cost_estimate=pl.CostEstimate(flops=flops, bytes_accessed=nbytes, transcendentals=0),
    )


def shape(rows, cols, dtype):
    return jax.ShapeDtypeStruct((rows, cols), dtype)


def to_x(a, k):
    return lax.ppermute(a, "x", [(i, (i + k) % NX) for i in range(NX)])


def along_z(a, k):
    pairs = [(z, (z + k) % NZ) for z in range(NZ)] + [(NZ + z, NZ + (z - k) % NZ) for z in range(NZ)]
    return lax.ppermute(a, ("core", "z"), pairs)


def to_core(a):
    return lax.ppermute(a, "core", [(0, 1), (1, 0)])


def cross(a):
    return lax.ppermute(a, ("yh", "yl"), [(0, 3), (3, 0), (1, 2), (2, 1)])


def at(i, size=BLK):
    return pl.ds(pl.multiple_of(i * size, size), size)


def back(i, k, n):
    return lax.rem(i - k + n, n)


def mask_kernel(pattern, density, sparse, *rest):
    *pieces, flags, block, sems = rest
    copies = [
        pltpu.make_async_copy(pattern, flags, sems.at[0]),
        pltpu.make_async_copy(density, block, sems.at[1]),
    ]
    for copy in copies:
        copy.start()
    for copy in copies:
        copy.wait()
    first = (lax.axis_index("yh") * 2 + lax.axis_index("core")) * 8
    column = lax.axis_index("z") * NX + lax.axis_index("x")
    for i in range(8):
        rows = slice(i * BLK, (i + 1) * BLK)
        value = block[rows, :]
        sparse[rows, :] = jnp.where(flags[first + i, column] == 1, value, jnp.zeros_like(value))
    x, yl = lax.axis_index("x"), lax.axis_index("yl")
    for k, piece in enumerate(pieces):
        piece[...] = sparse[at(yl * 4 + lax.rem(x + k, NX)), :]


def shard_kernel(*refs):
    *pieces, shard = refs
    x = lax.axis_index("x")
    for k, piece in enumerate(pieces):
        shard[:, at(back(x, k, NX))] = piece[...]


def panel_kernel(*refs):
    *blocks, panel = refs
    x = lax.axis_index("x")
    yh, core = lax.axis_index("yh"), lax.axis_index("core")
    for n, block in enumerate(blocks):
        k, dyh, dcore = n % 4, n // 4 % 2, n // 8
        group = lax.rem(yh + dyh, 2) * 2 + lax.rem(core + dcore, 2)
        panel[at(group, 1024), at(back(x, k, NX))] = block[...]


def join_cores_kernel(mine, other, both):
    core = lax.axis_index("core")
    both[at(core), :] = mine[...]
    both[at(1 - core), :] = other[...]


def split_kernel(both, *parts):
    core = lax.axis_index("core")
    parts[0][...] = both[at(1 - core), :]
    if len(parts) > 1:
        parts[1][...] = both[at(core), :]


def square_kernel(own, near2, near1, near3, far, back2, back1, back3, panel, square, half):
    core, z = lax.axis_index("core"), lax.axis_index("z")
    sign = 1 - 2 * core

    def part(lhs, k):
        owner = lax.rem(z - sign * k + NZ, NZ)
        return jnp.dot(lhs, panel[at(owner, 512), :], preferred_element_type=f32)

    total = part(own[...], 0)
    for k, ref in ((1, near1), (2, near2), (3, near3)):
        total += part(ref[at(core), :], k)
    for k, ref in ((-1, back1), (-2, back2), (-3, back3), (4, far)):
        total += part(ref[...], k)
    square[...] = total
    for k in range(NZ):
        half[k] = total.astype(bf16)


def cube_kernel(halves, panel, square, *rest):
    *pieces, total = rest
    cube = None
    for k in range(NZ):
        term = jnp.dot(halves[k], panel[k * 512 : (k + 1) * 512, :], preferred_element_type=f32)
        cube = term if cube is None else cube + term
    total[...] = 3.0 * square[...] - 2.0 * cube
    x = lax.axis_index("x")
    for k, piece in enumerate(pieces):
        piece[...] = total[:, at(lax.rem(x + k, NX))]


def join_kernel(*refs):
    *pieces, out = refs
    x = lax.axis_index("x")
    for k, piece in enumerate(pieces):
        out[at(back(x, k, NX)), :] = piece[...]


def gather_z(own):
    part = shape(BLK, 512, bf16)
    other = to_core(own)
    both = call(join_cores_kernel, shape(2 * BLK, 512, bf16), [VMEM] * 2)(own, other)
    near2 = along_z(both, 2)
    near1 = along_z(both, 1)
    near3 = along_z(near2, 1)
    send2, relay = call(split_kernel, [part] * 2, [VMEM])(near2)
    far = along_z(relay, 2)
    back2 = to_core(send2)
    back1 = to_core(call(split_kernel, [part], [VMEM])(near1)[0])
    back3 = to_core(call(split_kernel, [part], [VMEM])(near3)[0])
    return [own, near2, near1, near3, far, back2, back1, back3]


def step(density, pattern):
    piece = shape(BLK, BLK, bf16)
    own = [pltpu.SMEM((32, 32), jnp.int32), pltpu.VMEM((1024, BLK), bf16), pltpu.SemaphoreType.DMA((2,))]
    sparse, *pieces = call(mask_kernel, [shape(1024, BLK, bf16)] + [piece] * 4, [HBM] * 2, scratch=own)(pattern, density)
    pieces = [pieces[0]] + [to_x(pieces[k], k) for k in (1, 2, 3)]
    shard = call(shard_kernel, shape(BLK, 512, bf16), [VMEM] * 4)(*pieces)
    lefts = gather_z(shard)

    crossed = cross(sparse)
    blocks = [sparse] + [to_x(sparse, k) for k in (1, 2, 3)]
    far = cross(blocks[2])
    blocks = blocks + [crossed, to_x(crossed, 1), far, to_x(crossed, 3)]
    blocks = blocks + [to_core(b) for b in blocks]
    panel = call(panel_kernel, shape(4096, 512, bf16), [VMEM] * 16, nbytes=8 << 20)(*blocks)

    flops = 2 * 128 * 4096 * 512
    square, half = call(square_kernel, [shape(BLK, 512, f32), jax.ShapeDtypeStruct((NZ, BLK, 512), bf16)], [VMEM] * 9, flops, 5 << 20)(*lefts, panel)
    halves = lax.all_to_all(half, "z", 0, 0)
    pieces = call(cube_kernel, [shape(BLK, BLK, f32)] * 4, [VMEM] * 3, flops, 5 << 20, [pltpu.VMEM((BLK, 512), f32)])(halves, panel, square)
    pieces = [pieces[0]] + [to_x(pieces[k], k) for k in (1, 2, 3)]
    return call(join_kernel, shape(512, BLK, f32), [VMEM] * 4)(*pieces)


def solution(mesh):
    fine = Mesh(mesh.devices.reshape(2, 2, NZ, NX, 2), AXES)
    return jax.shard_map(
        step,
        mesh=fine,
        in_specs=(P(("yh", "core"), ("z", "x")), P()),
        out_specs=P(("yh", "core", "yl"), ("z", "x")),
        check_vma=False,
    )
```

```python
import jax
import jax.numpy as jnp
from jax import lax
from jax.experimental import pallas as pl
from jax.experimental.pallas import tpu as pltpu
from jax.sharding import Mesh, PartitionSpec as P


AXES = ("yh", "core", "z", "x", "yl")
NX, NZ = 4, 8
BLK = 128
VMEM = pl.BlockSpec(memory_space=pltpu.VMEM)
HBM = pl.BlockSpec(memory_space=pltpu.HBM)
bf16, f32 = jnp.bfloat16, jnp.float32
PARAMS = pltpu.CompilerParams(vmem_limit_bytes=16 << 20)


def call(kernel, outs, ins, flops=0, nbytes=0, scratch=()):
    return pl.pallas_call(
        kernel,
        out_shape=outs,
        in_specs=ins,
        out_specs=jax.tree.map(lambda _: VMEM, outs),
        scratch_shapes=scratch,
        compiler_params=PARAMS,
        cost_estimate=pl.CostEstimate(flops=flops, bytes_accessed=nbytes, transcendentals=0),
    )


def shape(rows, cols, dtype):
    return jax.ShapeDtypeStruct((rows, cols), dtype)


def to_x(a, k):
    return lax.ppermute(a, "x", [(i, (i + k) % NX) for i in range(NX)])


def along_z(a, k):
    pairs = [(z, (z + k) % NZ) for z in range(NZ)] + [(NZ + z, NZ + (z - k) % NZ) for z in range(NZ)]
    return lax.ppermute(a, ("core", "z"), pairs)


def along_x(a):
    pairs = [(x, (x + 1) % NX) for x in range(NX)] + [(NX + x, NX + (x - 1) % NX) for x in range(NX)]
    return lax.ppermute(a, ("core", "x"), pairs)


def to_core(a):
    return lax.ppermute(a, "core", [(0, 1), (1, 0)])


def cross(a):
    return lax.ppermute(a, ("yh", "yl"), [(0, 3), (3, 0), (1, 2), (2, 1)])


def at(i, size=BLK):
    return pl.ds(pl.multiple_of(i * size, size), size)


def back(i, k, n):
    return lax.rem(i - k + n, n)


def mask_kernel(pattern, density, sparse, *rest):
    *pieces, flags, block, sems = rest
    copies = [
        pltpu.make_async_copy(pattern, flags, sems.at[0]),
        pltpu.make_async_copy(density, block, sems.at[1]),
    ]
    for copy in copies:
        copy.start()
    for copy in copies:
        copy.wait()
    first = (lax.axis_index("yh") * 2 + lax.axis_index("core")) * 8
    column = lax.axis_index("z") * NX + lax.axis_index("x")
    for i in range(8):
        rows = slice(i * BLK, (i + 1) * BLK)
        value = block[rows, :]
        sparse[rows, :] = jnp.where(flags[first + i, column] == 1, value, jnp.zeros_like(value))
    x, yl = lax.axis_index("x"), lax.axis_index("yl")
    for k, piece in enumerate(pieces):
        piece[...] = sparse[at(yl * 4 + lax.rem(x + k, NX)), :]


def shard_kernel(*refs):
    *pieces, shard = refs
    x = lax.axis_index("x")
    for k, piece in enumerate(pieces):
        shard[:, at(back(x, k, NX))] = piece[...]


def panel_kernel(*refs):
    *blocks, panel = refs
    x, yh, core = lax.axis_index("x"), lax.axis_index("yh"), lax.axis_index("core")
    sign = 1 - 2 * core
    for n in range(2):
        own, near, away, far, other = blocks[5 * n : 5 * n + 5]
        half = lax.rem(yh + n, 2)
        rows = at(half, 2048)
        panel[rows, at(x)] = own[...]
        panel[rows, at(lax.rem(x - sign + NX, NX))] = near[...]
        panel[rows, at(lax.rem(x + sign + NX, NX))] = away[...]
        opposite = at(lax.rem(x + 2, NX))
        panel[at(half * 2 + core, 1024), opposite] = far[...]
        panel[at(half * 2 + 1 - core, 1024), opposite] = other[...]


def join_cores_kernel(mine, other, both):
    core, rows = lax.axis_index("core"), mine.shape[0]
    both[at(core, rows), :] = mine[...]
    both[at(1 - core, rows), :] = other[...]


def split_kernel(both, *parts):
    core, rows = lax.axis_index("core"), both.shape[0] // 2
    parts[0][...] = both[at(1 - core, rows), :]
    if len(parts) > 1:
        parts[1][...] = both[at(core, rows), :]


def mine_kernel(both, part):
    part[...] = both[at(lax.axis_index("core"), part.shape[0]), :]


def product(refs, panel):
    own, near2, near1, near3, far, back2, back1, back3 = refs
    core, z = lax.axis_index("core"), lax.axis_index("z")
    sign = 1 - 2 * core

    def part(lhs, k):
        owner = lax.rem(z - sign * k + NZ, NZ)
        return jnp.dot(lhs, panel[at(owner, 512), :], preferred_element_type=f32)

    total = part(own[...], 0)
    for k, ref in ((1, near1), (2, near2), (3, near3)):
        total += part(ref[at(core), :], k)
    for k, ref in ((-1, back1), (-2, back2), (-3, back3), (4, far)):
        total += part(ref[...], k)
    return total


def square_kernel(*refs):
    *lefts, panel, square, half = refs
    value = product(lefts, panel)
    square[...] = value
    half[...] = value.astype(bf16)


def cube_kernel(*refs):
    lefts, (panel, square), pieces, total = refs[:8], refs[8:10], refs[10:14], refs[14]
    total[...] = 3.0 * square[...] - 2.0 * product(lefts, panel)
    x = lax.axis_index("x")
    for k, piece in enumerate(pieces):
        piece[...] = total[:, at(lax.rem(x + k, NX))]


def join_kernel(*refs):
    *pieces, out = refs
    x = lax.axis_index("x")
    for k, piece in enumerate(pieces):
        out[at(back(x, k, NX)), :] = piece[...]


def gather_z(own):
    part = shape(BLK, 512, bf16)
    other = to_core(own)
    both = call(join_cores_kernel, shape(2 * BLK, 512, bf16), [VMEM] * 2)(own, other)
    near2 = along_z(both, 2)
    near1 = along_z(both, 1)
    near3 = along_z(near2, 1)
    send2, relay = call(split_kernel, [part] * 2, [VMEM])(near2)
    far = along_z(relay, 2)
    back2 = to_core(send2)
    back1 = to_core(call(split_kernel, [part], [VMEM])(near1)[0])
    back3 = to_core(call(split_kernel, [part], [VMEM])(near3)[0])
    return [own, near2, near1, near3, far, back2, back1, back3]


def gather_x(mine):
    other = to_core(mine)
    own = call(join_cores_kernel, shape(2048, BLK, bf16), [VMEM] * 2)(mine, other)
    near = along_x(own)
    far = along_x(call(mine_kernel, shape(1024, BLK, bf16), [VMEM])(near))
    return [own, near, to_core(near), far, to_core(far)]


def step(density, pattern):
    piece = shape(BLK, BLK, bf16)
    own = [pltpu.SMEM((32, 32), jnp.int32), pltpu.VMEM((1024, BLK), bf16), pltpu.SemaphoreType.DMA((2,))]
    sparse, *pieces = call(mask_kernel, [shape(1024, BLK, bf16)] + [piece] * 4, [HBM] * 2, scratch=own)(pattern, density)
    pieces = [pieces[0]] + [to_x(pieces[k], k) for k in (1, 2, 3)]
    shard = call(shard_kernel, shape(BLK, 512, bf16), [VMEM] * 4)(*pieces)
    lefts = gather_z(shard)

    crossed = cross(sparse)
    blocks = gather_x(sparse) + gather_x(crossed)
    panel = call(panel_kernel, shape(4096, 512, bf16), [VMEM] * 10, nbytes=8 << 20)(*blocks)

    flops = 2 * 128 * 4096 * 512
    square, half = call(square_kernel, [shape(BLK, 512, f32), shape(BLK, 512, bf16)], [VMEM] * 9, flops, 5 << 20)(*lefts, panel)
    lefts = gather_z(half)
    pieces = call(cube_kernel, [shape(BLK, BLK, f32)] * 4, [VMEM] * 10, flops, 5 << 20, [pltpu.VMEM((BLK, 512), f32)])(*lefts, panel, square)
    pieces = [pieces[0]] + [to_x(pieces[k], k) for k in (1, 2, 3)]
    return call(join_kernel, shape(512, BLK, f32), [VMEM] * 4)(*pieces)


def solution(mesh):
    fine = Mesh(mesh.devices.reshape(2, 2, NZ, NX, 2), AXES)
    return jax.shard_map(
        step,
        mesh=fine,
        in_specs=(P(("yh", "core"), ("z", "x")), P()),
        out_specs=P(("yh", "core", "yl"), ("z", "x")),
        check_vma=False,
    )
```

```python
import jax
import jax.numpy as jnp
from jax import lax
from jax.experimental import pallas as pl
from jax.experimental.pallas import tpu as pltpu
from jax.sharding import Mesh, PartitionSpec as P


AXES = ("yh", "core", "z", "x", "yl")
NX, NZ = 4, 8
BLK = 128
VMEM = pl.BlockSpec(memory_space=pltpu.VMEM)
HBM = pl.BlockSpec(memory_space=pltpu.HBM)
bf16, f32 = jnp.bfloat16, jnp.float32
PARAMS = pltpu.CompilerParams(vmem_limit_bytes=16 << 20)


def call(kernel, outs, ins, flops=0, nbytes=0, scratch=()):
    return pl.pallas_call(
        kernel,
        out_shape=outs,
        in_specs=ins,
        out_specs=jax.tree.map(lambda _: VMEM, outs),
        scratch_shapes=scratch,
        compiler_params=PARAMS,
        cost_estimate=pl.CostEstimate(flops=flops, bytes_accessed=nbytes, transcendentals=0),
    )


def shape(rows, cols, dtype):
    return jax.ShapeDtypeStruct((rows, cols), dtype)


def to_x(a, k):
    return lax.ppermute(a, "x", [(i, (i + k) % NX) for i in range(NX)])


def along_z(a, k):
    pairs = [(z, (z + k) % NZ) for z in range(NZ)] + [(NZ + z, NZ + (z - k) % NZ) for z in range(NZ)]
    return lax.ppermute(a, ("core", "z"), pairs)


def to_z(a, k):
    return lax.ppermute(a, "z", [(z, (z + k) % NZ) for z in range(NZ)])


def to_core(a):
    return lax.ppermute(a, "core", [(0, 1), (1, 0)])


def cross(a):
    return lax.ppermute(a, ("yh", "yl"), [(0, 3), (3, 0), (1, 2), (2, 1)])


def at(i, size=BLK):
    return pl.ds(pl.multiple_of(i * size, size), size)


def back(i, k, n):
    return lax.rem(i - k + n, n)


def mask_kernel(pattern, density, sparse, *rest):
    *pieces, flags, block, sems = rest
    copies = [
        pltpu.make_async_copy(pattern, flags, sems.at[0]),
        pltpu.make_async_copy(density, block, sems.at[1]),
    ]
    for copy in copies:
        copy.start()
    for copy in copies:
        copy.wait()
    first = (lax.axis_index("yh") * 2 + lax.axis_index("core")) * 8
    column = lax.axis_index("z") * NX + lax.axis_index("x")
    for i in range(8):
        rows = slice(i * BLK, (i + 1) * BLK)
        value = block[rows, :]
        sparse[rows, :] = jnp.where(flags[first + i, column] == 1, value, jnp.zeros_like(value))
    x, yl = lax.axis_index("x"), lax.axis_index("yl")
    for k, piece in enumerate(pieces):
        piece[...] = sparse[at(yl * 4 + lax.rem(x + k, NX)), :]


def shard_kernel(*refs):
    *pieces, shard = refs
    x = lax.axis_index("x")
    for k, piece in enumerate(pieces):
        shard[:, at(back(x, k, NX))] = piece[...]


def panel_kernel(*refs):
    *blocks, panel = refs
    x = lax.axis_index("x")
    yh, core = lax.axis_index("yh"), lax.axis_index("core")
    for n, block in enumerate(blocks):
        k, dyh, dcore = n % 4, n // 4 % 2, n // 8
        group = lax.rem(yh + dyh, 2) * 2 + lax.rem(core + dcore, 2)
        panel[at(group, 1024), at(back(x, k, NX))] = block[...]


def join_cores_kernel(mine, other, both):
    core = lax.axis_index("core")
    both[at(core), :] = mine[...]
    both[at(1 - core), :] = other[...]


def split_kernel(both, *parts):
    core = lax.axis_index("core")
    parts[0][...] = both[at(1 - core), :]
    if len(parts) > 1:
        parts[1][...] = both[at(core), :]


def term(lhs, k, panel):
    owner = lax.rem(lax.axis_index("z") - k + NZ, NZ)
    return jnp.dot(lhs, panel[at(owner, 512), :], preferred_element_type=f32)


def square_kernel(own, near2, near1, near3, far, back2, back1, back3, panel, square, half):
    core = lax.axis_index("core")
    sign = 1 - 2 * core
    total = term(own[...], 0, panel)
    for k, ref in ((1, near1), (2, near2), (3, near3)):
        total += term(ref[at(core), :], sign * k, panel)
    for k, ref in ((-1, back1), (-2, back2), (-3, back3), (4, far)):
        total += term(ref[...], sign * k, panel)
    square[...] = total
    half[...] = total.astype(bf16)


SHIFTS = (0, 1, -1, 2, -2, 3, -3, 4)


def cube_kernel(*refs):
    lefts, (panel, square), pieces, total = refs[:8], refs[8:10], refs[10:14], refs[14]
    cube = None
    for k, ref in zip(SHIFTS, lefts):
        part = term(ref[...], k, panel)
        cube = part if cube is None else cube + part
    total[...] = 3.0 * square[...] - 2.0 * cube
    x = lax.axis_index("x")
    for k, piece in enumerate(pieces):
        piece[...] = total[:, at(lax.rem(x + k, NX))]


def pick_kernel(first, second, out):
    out[...] = jnp.where(lax.axis_index("core") == 0, first[...], second[...])


def join_kernel(*refs):
    *pieces, out = refs
    x = lax.axis_index("x")
    for k, piece in enumerate(pieces):
        out[at(back(x, k, NX)), :] = piece[...]


def gather_z(own):
    part = shape(BLK, 512, bf16)
    other = to_core(own)
    both = call(join_cores_kernel, shape(2 * BLK, 512, bf16), [VMEM] * 2)(own, other)
    near2 = along_z(both, 2)
    near1 = along_z(both, 1)
    near3 = along_z(near2, 1)
    send2, relay = call(split_kernel, [part] * 2, [VMEM])(near2)
    far = along_z(relay, 2)
    back2 = to_core(send2)
    back1 = to_core(call(split_kernel, [part], [VMEM])(near1)[0])
    back3 = to_core(call(split_kernel, [part], [VMEM])(near3)[0])
    return [own, near2, near1, near3, far, back2, back1, back3]


def gather_z_apart(own):
    got = {0: own}
    for k in (2, -2, 1, -1):
        got[k] = to_z(own, k)
    got[4] = along_z(call(pick_kernel, shape(BLK, 512, bf16), [VMEM] * 2)(got[2], got[-2]), 2)
    got[3], got[-3] = to_z(got[2], 1), to_z(got[-2], -1)
    return [got[k] for k in SHIFTS]


def step(density, pattern):
    piece = shape(BLK, BLK, bf16)
    own = [pltpu.SMEM((32, 32), jnp.int32), pltpu.VMEM((1024, BLK), bf16), pltpu.SemaphoreType.DMA((2,))]
    sparse, *pieces = call(mask_kernel, [shape(1024, BLK, bf16)] + [piece] * 4, [HBM] * 2, scratch=own)(pattern, density)
    pieces = [pieces[0]] + [to_x(pieces[k], k) for k in (1, 2, 3)]
    shard = call(shard_kernel, shape(BLK, 512, bf16), [VMEM] * 4)(*pieces)
    lefts = gather_z(shard)

    crossed = cross(sparse)
    blocks = [sparse] + [to_x(sparse, k) for k in (1, 2, 3)]
    far = cross(blocks[2])
    blocks = blocks + [crossed, to_x(crossed, 1), far, to_x(crossed, 3)]
    blocks = blocks + [to_core(b) for b in blocks]
    panel = call(panel_kernel, shape(4096, 512, bf16), [VMEM] * 16, nbytes=8 << 20)(*blocks)

    flops = 2 * 128 * 4096 * 512
    square, half = call(square_kernel, [shape(BLK, 512, f32), shape(BLK, 512, bf16)], [VMEM] * 9, flops, 5 << 20)(*lefts, panel)
    lefts = gather_z_apart(half)
    pieces = call(cube_kernel, [shape(BLK, BLK, f32)] * 4, [VMEM] * 10, flops, 5 << 20, [pltpu.VMEM((BLK, 512), f32)])(*lefts, panel, square)
    pieces = [pieces[0]] + [to_x(pieces[k], k) for k in (1, 2, 3)]
    return call(join_kernel, shape(512, BLK, f32), [VMEM] * 4)(*pieces)


def solution(mesh):
    fine = Mesh(mesh.devices.reshape(2, 2, NZ, NX, 2), AXES)
    return jax.shard_map(
        step,
        mesh=fine,
        in_specs=(P(("yh", "core"), ("z", "x")), P()),
        out_specs=P(("yh", "core", "yl"), ("z", "x")),
        check_vma=False,
    )
```

```python
import jax
import jax.numpy as jnp
from jax import lax
from jax.experimental import pallas as pl
from jax.experimental.pallas import tpu as pltpu
from jax.sharding import Mesh, PartitionSpec as P


AXES = ("yh", "core", "z", "x", "yl")
NX, NZ = 4, 8
BLK = 128
VMEM = pl.BlockSpec(memory_space=pltpu.VMEM)
HBM = pl.BlockSpec(memory_space=pltpu.HBM)
bf16, f32 = jnp.bfloat16, jnp.float32
PARAMS = pltpu.CompilerParams(vmem_limit_bytes=16 << 20)


def call(kernel, outs, ins, flops=0, nbytes=0, scratch=()):
    return pl.pallas_call(
        kernel,
        out_shape=outs,
        in_specs=ins,
        out_specs=jax.tree.map(lambda _: VMEM, outs),
        scratch_shapes=scratch,
        compiler_params=PARAMS,
        cost_estimate=pl.CostEstimate(flops=flops, bytes_accessed=nbytes, transcendentals=0),
    )


def shape(rows, cols, dtype):
    return jax.ShapeDtypeStruct((rows, cols), dtype)


def to_x(a, k):
    return lax.ppermute(a, "x", [(i, (i + k) % NX) for i in range(NX)])


def along_z(a, k):
    pairs = [(z, (z + k) % NZ) for z in range(NZ)] + [(NZ + z, NZ + (z - k) % NZ) for z in range(NZ)]
    return lax.ppermute(a, ("core", "z"), pairs)


def to_z(a, k):
    return lax.ppermute(a, "z", [(z, (z + k) % NZ) for z in range(NZ)])


def to_core(a):
    return lax.ppermute(a, "core", [(0, 1), (1, 0)])


def cross(a):
    return lax.ppermute(a, ("yh", "yl"), [(0, 3), (3, 0), (1, 2), (2, 1)])


def at(i, size=BLK):
    return pl.ds(pl.multiple_of(i * size, size), size)


def back(i, k, n):
    return lax.rem(i - k + n, n)


def mask_kernel(pattern, density, sparse, *rest):
    *pieces, flags, block, sems = rest
    copies = [
        pltpu.make_async_copy(pattern, flags, sems.at[0]),
        pltpu.make_async_copy(density, block, sems.at[1]),
    ]
    for copy in copies:
        copy.start()
    for copy in copies:
        copy.wait()
    first = (lax.axis_index("yh") * 2 + lax.axis_index("core")) * 8
    column = lax.axis_index("z") * NX + lax.axis_index("x")
    for i in range(8):
        rows = slice(i * BLK, (i + 1) * BLK)
        value = block[rows, :]
        sparse[rows, :] = jnp.where(flags[first + i, column] == 1, value, jnp.zeros_like(value))
    x, yl = lax.axis_index("x"), lax.axis_index("yl")
    for k, piece in enumerate(pieces):
        piece[...] = sparse[at(yl * 4 + lax.rem(x + k, NX)), :]


def shard_kernel(*refs):
    *pieces, shard = refs
    x = lax.axis_index("x")
    for k, piece in enumerate(pieces):
        shard[:, at(back(x, k, NX))] = piece[...]


def panel_kernel(*refs):
    *blocks, panel = refs
    x = lax.axis_index("x")
    yh, core = lax.axis_index("yh"), lax.axis_index("core")
    for n, block in enumerate(blocks):
        k, dyh, dcore = n % 4, n // 4 % 2, n // 8
        group = lax.rem(yh + dyh, 2) * 2 + lax.rem(core + dcore, 2)
        panel[at(group, 1024), at(back(x, k, NX))] = block[...]


def join_cores_kernel(mine, other, both):
    core = lax.axis_index("core")
    both[at(core), :] = mine[...]
    both[at(1 - core), :] = other[...]


def split_kernel(both, *parts):
    core = lax.axis_index("core")
    parts[0][...] = both[at(1 - core), :]
    if len(parts) > 1:
        parts[1][...] = both[at(core), :]


def term(lhs, k, panel):
    owner = lax.rem(lax.axis_index("z") - k + NZ, NZ)
    return jnp.dot(lhs, panel[at(owner, 512), :], preferred_element_type=f32)


def square_kernel(own, near2, near1, near3, far, back2, back1, back3, panel, square, half):
    core = lax.axis_index("core")
    sign = 1 - 2 * core
    total = term(own[...], 0, panel)
    for k, ref in ((1, near1), (2, near2), (3, near3)):
        total += term(ref[at(core), :], sign * k, panel)
    for k, ref in ((-1, back1), (-2, back2), (-3, back3), (4, far)):
        total += term(ref[...], sign * k, panel)
    square[...] = total
    half[...] = total.astype(bf16)


SHIFTS = (0, 1, -1, 2, -2, 3, -3, 4)


def cube_kernel(*refs):
    lefts, (panel, square), pieces, total = refs[:8], refs[8:10], refs[10:14], refs[14]
    cube = None
    for k, ref in zip(SHIFTS, lefts):
        part = term(ref[...], k, panel)
        cube = part if cube is None else cube + part
    total[...] = 3.0 * square[...] - 2.0 * cube
    x = lax.axis_index("x")
    for k, piece in enumerate(pieces):
        piece[...] = total[:, at(lax.rem(x + k, NX))]


def pick_kernel(first, second, out):
    out[...] = jnp.where(lax.axis_index("core") == 0, first[...], second[...])


def join_kernel(*refs):
    *pieces, out = refs
    x = lax.axis_index("x")
    for k, piece in enumerate(pieces):
        out[at(back(x, k, NX)), :] = piece[...]


def gather_z(own):
    part = shape(BLK, 512, bf16)
    other = to_core(own)
    both = call(join_cores_kernel, shape(2 * BLK, 512, bf16), [VMEM] * 2)(own, other)
    near1 = along_z(both, 1)
    near2 = along_z(near1, 1)
    near3 = along_z(near2, 1)
    send2, relay = call(split_kernel, [part] * 2, [VMEM])(near2)
    far = along_z(relay, 2)
    back1 = to_core(call(split_kernel, [part], [VMEM])(near1)[0])
    back2 = to_core(send2)
    back3 = to_core(call(split_kernel, [part], [VMEM])(near3)[0])
    return [own, near2, near1, near3, far, back2, back1, back3]


def gather_z_apart(own):
    got = {0: own}
    for k in (1, 2, 3):
        for sign in (1, -1):
            got[sign * k] = to_z(got[sign * (k - 1)], sign)
    got[4] = along_z(call(pick_kernel, shape(BLK, 512, bf16), [VMEM] * 2)(got[2], got[-2]), 2)
    return [got[k] for k in SHIFTS]


def step(density, pattern):
    piece = shape(BLK, BLK, bf16)
    own = [pltpu.SMEM((32, 32), jnp.int32), pltpu.VMEM((1024, BLK), bf16), pltpu.SemaphoreType.DMA((2,))]
    sparse, *pieces = call(mask_kernel, [shape(1024, BLK, bf16)] + [piece] * 4, [HBM] * 2, scratch=own)(pattern, density)
    pieces = [pieces[0]] + [to_x(pieces[k], k) for k in (1, 2, 3)]
    shard = call(shard_kernel, shape(BLK, 512, bf16), [VMEM] * 4)(*pieces)
    lefts = gather_z(shard)

    crossed = cross(sparse)
    blocks = [sparse] + [to_x(sparse, k) for k in (1, 2, 3)]
    far = cross(blocks[2])
    blocks = blocks + [crossed, to_x(crossed, 1), far, to_x(crossed, 3)]
    blocks = blocks + [to_core(b) for b in blocks]
    panel = call(panel_kernel, shape(4096, 512, bf16), [VMEM] * 16, nbytes=8 << 20)(*blocks)

    flops = 2 * 128 * 4096 * 512
    square, half = call(square_kernel, [shape(BLK, 512, f32), shape(BLK, 512, bf16)], [VMEM] * 9, flops, 5 << 20)(*lefts, panel)
    lefts = gather_z_apart(half)
    pieces = call(cube_kernel, [shape(BLK, BLK, f32)] * 4, [VMEM] * 10, flops, 5 << 20, [pltpu.VMEM((BLK, 512), f32)])(*lefts, panel, square)
    pieces = [pieces[0]] + [to_x(pieces[k], k) for k in (1, 2, 3)]
    return call(join_kernel, shape(512, BLK, f32), [VMEM] * 4)(*pieces)


def solution(mesh):
    fine = Mesh(mesh.devices.reshape(2, 2, NZ, NX, 2), AXES)
    return jax.shard_map(
        step,
        mesh=fine,
        in_specs=(P(("yh", "core"), ("z", "x")), P()),
        out_specs=P(("yh", "core", "yl"), ("z", "x")),
        check_vma=False,
    )
```

```python
import jax
import jax.numpy as jnp
from jax import lax
from jax.experimental import pallas as pl
from jax.experimental.pallas import tpu as pltpu
from jax.sharding import Mesh, PartitionSpec as P


AXES = ("yh", "core", "z", "x", "yl")
NX, NZ = 4, 8
BLK = 128
VMEM = pl.BlockSpec(memory_space=pltpu.VMEM)
HBM = pl.BlockSpec(memory_space=pltpu.HBM)
bf16, f32 = jnp.bfloat16, jnp.float32
PARAMS = pltpu.CompilerParams(vmem_limit_bytes=16 << 20)


def call(kernel, outs, ins, flops=0, nbytes=0, scratch=()):
    return pl.pallas_call(
        kernel,
        out_shape=outs,
        in_specs=ins,
        out_specs=jax.tree.map(lambda _: VMEM, outs),
        scratch_shapes=scratch,
        compiler_params=PARAMS,
        cost_estimate=pl.CostEstimate(flops=flops, bytes_accessed=nbytes, transcendentals=0),
    )


def shape(rows, cols, dtype):
    return jax.ShapeDtypeStruct((rows, cols), dtype)


def to_x(a, k):
    return lax.ppermute(a, "x", [(i, (i + k) % NX) for i in range(NX)])


def along_z(a, k):
    pairs = [(z, (z + k) % NZ) for z in range(NZ)] + [(NZ + z, NZ + (z - k) % NZ) for z in range(NZ)]
    return lax.ppermute(a, ("core", "z"), pairs)


def to_z(a, k):
    return lax.ppermute(a, "z", [(z, (z + k) % NZ) for z in range(NZ)])


def to_core(a):
    return lax.ppermute(a, "core", [(0, 1), (1, 0)])


def cross(a):
    return lax.ppermute(a, ("yh", "yl"), [(0, 3), (3, 0), (1, 2), (2, 1)])


def at(i, size=BLK):
    return pl.ds(pl.multiple_of(i * size, size), size)


def back(i, k, n):
    return lax.rem(i - k + n, n)


def mask_kernel(pattern, density, sparse, crossed_flags, *rest):
    *pieces, flags, block, sems = rest
    copies = [
        pltpu.make_async_copy(pattern, flags, sems.at[0]),
        pltpu.make_async_copy(density, block, sems.at[1]),
    ]
    for copy in copies:
        copy.start()
    for copy in copies:
        copy.wait()
    yh, core = lax.axis_index("yh"), lax.axis_index("core")
    column = lax.axis_index("z") * NX + lax.axis_index("x")
    for i in range(8):
        rows = slice(i * BLK, (i + 1) * BLK)
        value = block[rows, :]
        sparse[rows, :] = jnp.where(flags[(yh * 2 + core) * 8 + i, column] == 1, value, jnp.zeros_like(value))
        flag = flags[((1 - yh) * 2 + core) * 8 + i, column]
        crossed_flags[i * 8 : i * 8 + 8, :] = jnp.broadcast_to(flag, (8, BLK)).astype(jnp.int32)
    x, yl = lax.axis_index("x"), lax.axis_index("yl")
    for k, piece in enumerate(pieces):
        piece[...] = sparse[at(yl * 4 + lax.rem(x + k, NX)), :]


def mask_crossed_kernel(flags, block, out):
    for i in range(8):
        rows = slice(i * BLK, (i + 1) * BLK)
        value = block[rows, :]
        keep = jnp.broadcast_to(flags[i * 8 : i * 8 + 1, :], (BLK, BLK)) == 1
        out[rows, :] = jnp.where(keep, value.astype(f32), 0.0).astype(bf16)


def shard_kernel(*refs):
    *pieces, shard = refs
    x = lax.axis_index("x")
    for k, piece in enumerate(pieces):
        shard[:, at(back(x, k, NX))] = piece[...]


def half_kernel(*refs):
    *blocks, half = refs
    x = lax.axis_index("x")
    for k, block in enumerate(blocks):
        half[:, at(back(x, k, NX))] = block[...]


def panel_kernel(*refs):
    mine, theirs, *blocks, panel = refs
    x, yh, core = lax.axis_index("x"), lax.axis_index("yh"), lax.axis_index("core")
    panel[at(yh * 2 + core, 1024), :] = mine[...]
    panel[at(yh * 2 + 1 - core, 1024), :] = theirs[...]
    for n, block in enumerate(blocks):
        k, dcore = n % 4, n // 4
        group = (1 - yh) * 2 + lax.rem(core + dcore, 2)
        panel[at(group, 1024), at(back(x, k, NX))] = block[...]


def join_cores_kernel(mine, other, both):
    core = lax.axis_index("core")
    both[at(core), :] = mine[...]
    both[at(1 - core), :] = other[...]


def split_kernel(both, *parts):
    core = lax.axis_index("core")
    parts[0][...] = both[at(1 - core), :]
    if len(parts) > 1:
        parts[1][...] = both[at(core), :]


def term(lhs, k, panel):
    owner = lax.rem(lax.axis_index("z") - k + NZ, NZ)
    return jnp.dot(lhs, panel[at(owner, 512), :], preferred_element_type=f32)


def square_kernel(own, near2, near1, near3, far, back2, back1, back3, panel, square, half):
    core = lax.axis_index("core")
    sign = 1 - 2 * core
    total = term(own[...], 0, panel)
    for k, ref in ((1, near1), (2, near2), (3, near3)):
        total += term(ref[at(core), :], sign * k, panel)
    for k, ref in ((-1, back1), (-2, back2), (-3, back3), (4, far)):
        total += term(ref[...], sign * k, panel)
    square[...] = total
    half[...] = total.astype(bf16)


SHIFTS = (0, 1, -1, 2, -2, 3, -3, 4)


def cube_kernel(*refs):
    lefts, (panel, square), pieces, total = refs[:8], refs[8:10], refs[10:14], refs[14]
    cube = None
    for k, ref in zip(SHIFTS, lefts):
        part = term(ref[...], k, panel)
        cube = part if cube is None else cube + part
    total[...] = 3.0 * square[...] - 2.0 * cube
    x = lax.axis_index("x")
    for k, piece in enumerate(pieces):
        piece[...] = total[:, at(lax.rem(x + k, NX))]


def pick_kernel(first, second, out):
    out[...] = jnp.where(lax.axis_index("core") == 0, first[...], second[...])


def join_kernel(*refs):
    *pieces, out = refs
    x = lax.axis_index("x")
    for k, piece in enumerate(pieces):
        out[at(back(x, k, NX)), :] = piece[...]


def gather_z(own):
    part = shape(BLK, 512, bf16)
    other = to_core(own)
    both = call(join_cores_kernel, shape(2 * BLK, 512, bf16), [VMEM] * 2)(own, other)
    near2 = along_z(both, 2)
    near1 = along_z(both, 1)
    near3 = along_z(near2, 1)
    send2, relay = call(split_kernel, [part] * 2, [VMEM])(near2)
    far = along_z(relay, 2)
    back2 = to_core(send2)
    back1 = to_core(call(split_kernel, [part], [VMEM])(near1)[0])
    back3 = to_core(call(split_kernel, [part], [VMEM])(near3)[0])
    return [own, near2, near1, near3, far, back2, back1, back3]


def gather_z_apart(own):
    got = {0: own}
    for k in (2, -2, 1, -1):
        got[k] = to_z(own, k)
    got[4] = along_z(call(pick_kernel, shape(BLK, 512, bf16), [VMEM] * 2)(got[2], got[-2]), 2)
    got[3], got[-3] = to_z(got[2], 1), to_z(got[-2], -1)
    return [got[k] for k in SHIFTS]


def step(density, pattern):
    piece, block = shape(BLK, BLK, bf16), shape(1024, BLK, bf16)
    raw = cross(density)
    own = [pltpu.SMEM((32, 32), jnp.int32), pltpu.VMEM((1024, BLK), bf16), pltpu.SemaphoreType.DMA((2,))]
    outs = [block, shape(64, BLK, jnp.int32)] + [piece] * 4
    sparse, flags, *pieces = call(mask_kernel, outs, [HBM] * 2, scratch=own)(pattern, density)
    pieces = [pieces[0]] + [to_x(pieces[k], k) for k in (1, 2, 3)]
    shard = call(shard_kernel, shape(BLK, 512, bf16), [VMEM] * 4)(*pieces)
    lefts = gather_z(shard)

    blocks = [sparse] + [to_x(sparse, k) for k in (1, 2, 3)]
    mine = call(half_kernel, shape(1024, 512, bf16), [VMEM] * 4)(*blocks)
    theirs = to_core(mine)
    crossed = call(mask_crossed_kernel, block, [VMEM] * 2)(flags, raw)
    far = cross(blocks[2])
    blocks = [crossed, to_x(crossed, 1), far, to_x(crossed, 3)]
    blocks = blocks + [to_core(b) for b in blocks]
    panel = call(panel_kernel, shape(4096, 512, bf16), [VMEM] * 10, nbytes=8 << 20)(mine, theirs, *blocks)

    flops = 2 * 128 * 4096 * 512
    square, half = call(square_kernel, [shape(BLK, 512, f32), shape(BLK, 512, bf16)], [VMEM] * 9, flops, 5 << 20)(*lefts, panel)
    lefts = gather_z_apart(half)
    pieces = call(cube_kernel, [shape(BLK, BLK, f32)] * 4, [VMEM] * 10, flops, 5 << 20, [pltpu.VMEM((BLK, 512), f32)])(*lefts, panel, square)
    pieces = [pieces[0]] + [to_x(pieces[k], k) for k in (1, 2, 3)]
    return call(join_kernel, shape(512, BLK, f32), [VMEM] * 4)(*pieces)


def solution(mesh):
    fine = Mesh(mesh.devices.reshape(2, 2, NZ, NX, 2), AXES)
    return jax.shard_map(
        step,
        mesh=fine,
        in_specs=(P(("yh", "core"), ("z", "x")), P()),
        out_specs=P(("yh", "core", "yl"), ("z", "x")),
        check_vma=False,
    )
```

```python
import jax
import jax.numpy as jnp
from jax import lax
from jax.experimental import pallas as pl
from jax.experimental.pallas import tpu as pltpu
from jax.sharding import Mesh, PartitionSpec as P


AXES = ("yh", "core", "z", "x", "yl")
NX, NZ = 4, 8
BLK = 128
VMEM = pl.BlockSpec(memory_space=pltpu.VMEM)
HBM = pl.BlockSpec(memory_space=pltpu.HBM)
bf16, f32 = jnp.bfloat16, jnp.float32
PARAMS = pltpu.CompilerParams(vmem_limit_bytes=16 << 20)


def call(kernel, outs, ins, flops=0, nbytes=0, scratch=()):
    return pl.pallas_call(
        kernel,
        out_shape=outs,
        in_specs=ins,
        out_specs=jax.tree.map(lambda _: VMEM, outs),
        scratch_shapes=scratch,
        compiler_params=PARAMS,
        cost_estimate=pl.CostEstimate(flops=flops, bytes_accessed=nbytes, transcendentals=0),
    )


def shape(rows, cols, dtype):
    return jax.ShapeDtypeStruct((rows, cols), dtype)


def to_x(a, k):
    return lax.ppermute(a, "x", [(i, (i + k) % NX) for i in range(NX)])


def along_z(a, k):
    pairs = [(z, (z + k) % NZ) for z in range(NZ)] + [(NZ + z, NZ + (z - k) % NZ) for z in range(NZ)]
    return lax.ppermute(a, ("core", "z"), pairs)


def to_z(a, k):
    return lax.ppermute(a, "z", [(z, (z + k) % NZ) for z in range(NZ)])


def to_core(a):
    return lax.ppermute(a, "core", [(0, 1), (1, 0)])


def cross(a):
    return lax.ppermute(a, ("yh", "yl"), [(0, 3), (3, 0), (1, 2), (2, 1)])


def at(i, size=BLK):
    return pl.ds(pl.multiple_of(i * size, size), size)


def back(i, k, n):
    return lax.rem(i - k + n, n)


def mask_kernel(pattern, density, sparse, crossed_flags, *rest):
    *pieces, flags, block, sems = rest
    copies = [
        pltpu.make_async_copy(pattern, flags, sems.at[0]),
        pltpu.make_async_copy(density, block, sems.at[1]),
    ]
    for copy in copies:
        copy.start()
    for copy in copies:
        copy.wait()
    yh, core = lax.axis_index("yh"), lax.axis_index("core")
    column = lax.axis_index("z") * NX + lax.axis_index("x")
    for i in range(8):
        rows = slice(i * BLK, (i + 1) * BLK)
        value = block[rows, :]
        sparse[rows, :] = jnp.where(flags[(yh * 2 + core) * 8 + i, column] == 1, value, jnp.zeros_like(value))
        flag = flags[((1 - yh) * 2 + core) * 8 + i, column]
        crossed_flags[i * 8 : i * 8 + 8, :] = jnp.broadcast_to(flag, (8, BLK)).astype(jnp.int32)
    x, yl = lax.axis_index("x"), lax.axis_index("yl")
    for k, piece in enumerate(pieces):
        piece[...] = sparse[at(yl * 4 + lax.rem(x + k, NX)), :]


def mask_crossed_kernel(flags, block, out):
    for i in range(8):
        rows = slice(i * BLK, (i + 1) * BLK)
        value = block[rows, :]
        keep = jnp.broadcast_to(flags[i * 8 : i * 8 + 1, :], (BLK, BLK)) == 1
        out[rows, :] = jnp.where(keep, value.astype(f32), 0.0).astype(bf16)


def shard_kernel(*refs):
    *pieces, shard = refs
    x = lax.axis_index("x")
    for k, piece in enumerate(pieces):
        shard[:, at(back(x, k, NX))] = piece[...]


def half_kernel(*refs):
    *blocks, half = refs
    x = lax.axis_index("x")
    for k, block in enumerate(blocks):
        half[:, at(back(x, k, NX))] = block[...]


def panel_kernel(*refs):
    mine, theirs, *blocks, panel = refs
    x, yh, core = lax.axis_index("x"), lax.axis_index("yh"), lax.axis_index("core")
    panel[at(yh * 2 + core, 1024), :] = mine[...]
    panel[at(yh * 2 + 1 - core, 1024), :] = theirs[...]
    for n, block in enumerate(blocks):
        k, dcore = n % 4, n // 4
        group = (1 - yh) * 2 + lax.rem(core + dcore, 2)
        panel[at(group, 1024), at(back(x, k, NX))] = block[...]


def join_cores_kernel(mine, other, both):
    core = lax.axis_index("core")
    both[at(core), :] = mine[...]
    both[at(1 - core), :] = other[...]


def split_kernel(both, *parts):
    core = lax.axis_index("core")
    parts[0][...] = both[at(1 - core), :]
    if len(parts) > 1:
        parts[1][...] = both[at(core), :]


def term(lhs, k, panel):
    owner = lax.rem(lax.axis_index("z") - k + NZ, NZ)
    return jnp.dot(lhs, panel[at(owner, 512), :], preferred_element_type=f32)


def square_kernel(own, near2, near1, near3, far, back2, back1, back3, panel, square, half):
    core = lax.axis_index("core")
    sign = 1 - 2 * core
    total = term(own[...], 0, panel)
    for k, ref in ((1, near1), (2, near2), (3, near3)):
        total += term(ref[at(core), :], sign * k, panel)
    for k, ref in ((-1, back1), (-2, back2), (-3, back3), (4, far)):
        total += term(ref[...], sign * k, panel)
    square[...] = total
    half[...] = total.astype(bf16)


SHIFTS = (0, 1, -1, 2, -2, 3, -3, 4)


def early_kernel(*refs):
    *lefts, panel, cube = refs
    total = None
    for k, ref in zip(SHIFTS, lefts):
        part = term(ref[...], k, panel)
        total = part if total is None else total + part
    cube[...] = total


def cube_kernel(*refs):
    lefts, (panel, square, cube), pieces, total = refs[:3], refs[3:6], refs[6:10], refs[10]
    late = cube[...]
    for k, ref in zip(SHIFTS[5:], lefts):
        late += term(ref[...], k, panel)
    total[...] = 3.0 * square[...] - 2.0 * late
    x = lax.axis_index("x")
    for k, piece in enumerate(pieces):
        piece[...] = total[:, at(lax.rem(x + k, NX))]


def pick_kernel(first, second, out):
    out[...] = jnp.where(lax.axis_index("core") == 0, first[...], second[...])


def join_kernel(*refs):
    *pieces, out = refs
    x = lax.axis_index("x")
    for k, piece in enumerate(pieces):
        out[at(back(x, k, NX)), :] = piece[...]


def gather_z(own):
    part = shape(BLK, 512, bf16)
    other = to_core(own)
    both = call(join_cores_kernel, shape(2 * BLK, 512, bf16), [VMEM] * 2)(own, other)
    near2 = along_z(both, 2)
    near1 = along_z(both, 1)
    near3 = along_z(near2, 1)
    send2, relay = call(split_kernel, [part] * 2, [VMEM])(near2)
    far = along_z(relay, 2)
    back2 = to_core(send2)
    back1 = to_core(call(split_kernel, [part], [VMEM])(near1)[0])
    back3 = to_core(call(split_kernel, [part], [VMEM])(near3)[0])
    return [own, near2, near1, near3, far, back2, back1, back3]


def gather_z_apart(own):
    got = {0: own}
    for k in (2, -2, 1, -1):
        got[k] = to_z(own, k)
    got[4] = along_z(call(pick_kernel, shape(BLK, 512, bf16), [VMEM] * 2)(got[2], got[-2]), 2)
    got[3], got[-3] = to_z(got[2], 1), to_z(got[-2], -1)
    return [got[k] for k in SHIFTS]


def step(density, pattern):
    piece, block = shape(BLK, BLK, bf16), shape(1024, BLK, bf16)
    raw = cross(density)
    own = [pltpu.SMEM((32, 32), jnp.int32), pltpu.VMEM((1024, BLK), bf16), pltpu.SemaphoreType.DMA((2,))]
    outs = [block, shape(64, BLK, jnp.int32)] + [piece] * 4
    sparse, flags, *pieces = call(mask_kernel, outs, [HBM] * 2, scratch=own)(pattern, density)
    pieces = [pieces[0]] + [to_x(pieces[k], k) for k in (1, 2, 3)]
    shard = call(shard_kernel, shape(BLK, 512, bf16), [VMEM] * 4)(*pieces)
    lefts = gather_z(shard)

    blocks = [sparse] + [to_x(sparse, k) for k in (1, 2, 3)]
    mine = call(half_kernel, shape(1024, 512, bf16), [VMEM] * 4)(*blocks)
    theirs = to_core(mine)
    crossed = call(mask_crossed_kernel, block, [VMEM] * 2)(flags, raw)
    far = cross(blocks[2])
    blocks = [crossed, to_x(crossed, 1), far, to_x(crossed, 3)]
    blocks = blocks + [to_core(b) for b in blocks]
    panel = call(panel_kernel, shape(4096, 512, bf16), [VMEM] * 10, nbytes=8 << 20)(mine, theirs, *blocks)

    flops = 2 * 128 * 4096 * 512
    square, half = call(square_kernel, [shape(BLK, 512, f32), shape(BLK, 512, bf16)], [VMEM] * 9, flops, 5 << 20)(*lefts, panel)
    lefts = gather_z_apart(half)
    early = call(early_kernel, shape(BLK, 512, f32), [VMEM] * 6, flops, 5 << 20)(*lefts[:5], panel)
    pieces = call(cube_kernel, [shape(BLK, BLK, f32)] * 4, [VMEM] * 6, flops, 5 << 20, [pltpu.VMEM((BLK, 512), f32)])(*lefts[5:], panel, square, early)
    pieces = [pieces[0]] + [to_x(pieces[k], k) for k in (1, 2, 3)]
    return call(join_kernel, shape(512, BLK, f32), [VMEM] * 4)(*pieces)


def solution(mesh):
    fine = Mesh(mesh.devices.reshape(2, 2, NZ, NX, 2), AXES)
    return jax.shard_map(
        step,
        mesh=fine,
        in_specs=(P(("yh", "core"), ("z", "x")), P()),
        out_specs=P(("yh", "core", "yl"), ("z", "x")),
        check_vma=False,
    )
```

```python
import jax
import jax.numpy as jnp
from jax import lax
from jax.experimental import pallas as pl
from jax.experimental.pallas import tpu as pltpu
from jax.sharding import Mesh, PartitionSpec as P


AXES = ("yh", "core", "z", "x", "yl")
NX, NZ = 4, 8
BLK = 128
VMEM = pl.BlockSpec(memory_space=pltpu.VMEM)
HBM = pl.BlockSpec(memory_space=pltpu.HBM)
bf16, f32 = jnp.bfloat16, jnp.float32
PARAMS = pltpu.CompilerParams(vmem_limit_bytes=16 << 20)
WIDE = pltpu.CompilerParams(vmem_limit_bytes=63 << 20)


def call(kernel, outs, ins, flops=0, nbytes=0, scratch=(), params=PARAMS):
    return pl.pallas_call(
        kernel,
        out_shape=outs,
        in_specs=ins,
        out_specs=jax.tree.map(lambda _: VMEM, outs),
        scratch_shapes=scratch,
        compiler_params=params,
        cost_estimate=pl.CostEstimate(flops=flops, bytes_accessed=nbytes, transcendentals=0),
    )


def shape(rows, cols, dtype):
    return jax.ShapeDtypeStruct((rows, cols), dtype)


def to_x(a, k):
    return lax.ppermute(a, "x", [(i, (i + k) % NX) for i in range(NX)])


def along_z(a, k):
    pairs = [(z, (z + k) % NZ) for z in range(NZ)] + [(NZ + z, NZ + (z - k) % NZ) for z in range(NZ)]
    return lax.ppermute(a, ("core", "z"), pairs)


def to_z(a, k):
    return lax.ppermute(a, "z", [(z, (z + k) % NZ) for z in range(NZ)])


def to_core(a):
    return lax.ppermute(a, "core", [(0, 1), (1, 0)])


def cross(a):
    return lax.ppermute(a, ("yh", "yl"), [(0, 3), (3, 0), (1, 2), (2, 1)])


def at(i, size=BLK):
    return pl.ds(pl.multiple_of(i * size, size), size)


def back(i, k, n):
    return lax.rem(i - k + n, n)


def mask_kernel(pattern, density, sparse, crossed_flags, *rest):
    *pieces, flags, block, sems = rest
    copies = [
        pltpu.make_async_copy(pattern, flags, sems.at[0]),
        pltpu.make_async_copy(density, block, sems.at[1]),
    ]
    for copy in copies:
        copy.start()
    for copy in copies:
        copy.wait()
    yh, core = lax.axis_index("yh"), lax.axis_index("core")
    column = lax.axis_index("z") * NX + lax.axis_index("x")
    for i in range(8):
        rows = slice(i * BLK, (i + 1) * BLK)
        value = block[rows, :]
        sparse[rows, :] = jnp.where(flags[(yh * 2 + core) * 8 + i, column] == 1, value, jnp.zeros_like(value))
        flag = flags[((1 - yh) * 2 + core) * 8 + i, column]
        crossed_flags[i * 8 : i * 8 + 8, :] = jnp.broadcast_to(flag, (8, BLK)).astype(jnp.int32)
    x, yl = lax.axis_index("x"), lax.axis_index("yl")
    for k, piece in enumerate(pieces):
        piece[...] = sparse[at(yl * 4 + lax.rem(x + k, NX)), :]


def mask_crossed_kernel(flags, block, out):
    for i in range(8):
        rows = slice(i * BLK, (i + 1) * BLK)
        value = block[rows, :]
        keep = jnp.broadcast_to(flags[i * 8 : i * 8 + 1, :], (BLK, BLK)) == 1
        out[rows, :] = jnp.where(keep, value.astype(f32), 0.0).astype(bf16)


def shard_kernel(*refs):
    *pieces, shard = refs
    x = lax.axis_index("x")
    for k, piece in enumerate(pieces):
        shard[:, at(back(x, k, NX))] = piece[...]


def half_kernel(*refs):
    *blocks, half = refs
    x = lax.axis_index("x")
    for k, block in enumerate(blocks):
        half[:, at(back(x, k, NX))] = block[...]


def panel_kernel(*refs):
    mine, theirs, *blocks, panel = refs
    x, yh, core = lax.axis_index("x"), lax.axis_index("yh"), lax.axis_index("core")
    panel[at(yh * 2 + core, 1024), :] = mine[...]
    panel[at(yh * 2 + 1 - core, 1024), :] = theirs[...]
    for n, block in enumerate(blocks):
        k, dcore = n % 4, n // 4
        group = (1 - yh) * 2 + lax.rem(core + dcore, 2)
        panel[at(group, 1024), at(back(x, k, NX))] = block[...]


def join_cores_kernel(mine, other, both):
    core = lax.axis_index("core")
    both[at(core), :] = mine[...]
    both[at(1 - core), :] = other[...]


def split_kernel(both, *parts):
    core = lax.axis_index("core")
    parts[0][...] = both[at(1 - core), :]
    if len(parts) > 1:
        parts[1][...] = both[at(core), :]


def term(lhs, k, panel):
    owner = lax.rem(lax.axis_index("z") - k + NZ, NZ)
    return jnp.dot(lhs, panel[at(owner, 512), :], preferred_element_type=f32)


def square_kernel(own, near2, near1, near3, far, back2, back1, back3, panel, square, half):
    core = lax.axis_index("core")
    sign = 1 - 2 * core
    total = term(own[...], 0, panel)
    for k, ref in ((1, near1), (2, near2), (3, near3)):
        total += term(ref[at(core), :], sign * k, panel)
    for k, ref in ((-1, back1), (-2, back2), (-3, back3), (4, far)):
        total += term(ref[...], sign * k, panel)
    square[...] = total
    half[...] = total.astype(bf16)


SHIFTS = (0, 1, -1, 2, -2, 3, -3, 4)


def early_kernel(*refs):
    *lefts, panel, cube = refs
    total = None
    for k, ref in zip(SHIFTS, lefts):
        part = term(ref[...], k, panel)
        total = part if total is None else total + part
    cube[...] = total


def cube_kernel(*refs):
    lefts, (panel, square, cube), pieces, total = refs[:3], refs[3:6], refs[6:10], refs[10]
    late = cube[...]
    for k, ref in zip(SHIFTS[5:], lefts):
        late += term(ref[...], k, panel)
    total[...] = 3.0 * square[...] - 2.0 * late
    x = lax.axis_index("x")
    for k, piece in enumerate(pieces):
        piece[...] = total[:, at(lax.rem(x + k, NX))]


def pick_kernel(first, second, out):
    out[...] = jnp.where(lax.axis_index("core") == 0, first[...], second[...])


def join_kernel(*refs):
    *pieces, out = refs
    x = lax.axis_index("x")
    for k, piece in enumerate(pieces):
        out[at(back(x, k, NX)), :] = piece[...]


def gather_z(own):
    part = shape(BLK, 512, bf16)
    other = to_core(own)
    both = call(join_cores_kernel, shape(2 * BLK, 512, bf16), [VMEM] * 2)(own, other)
    near2 = along_z(both, 2)
    near1 = along_z(both, 1)
    near3 = along_z(near2, 1)
    send2, relay = call(split_kernel, [part] * 2, [VMEM])(near2)
    far = along_z(relay, 2)
    back2 = to_core(send2)
    back1 = to_core(call(split_kernel, [part], [VMEM])(near1)[0])
    back3 = to_core(call(split_kernel, [part], [VMEM])(near3)[0])
    return [own, near2, near1, near3, far, back2, back1, back3]


def gather_z_apart(own):
    got = {0: own}
    for k in (2, -2, 1, -1):
        got[k] = to_z(own, k)
    got[4] = along_z(call(pick_kernel, shape(BLK, 512, bf16), [VMEM] * 2)(got[2], got[-2]), 2)
    got[3], got[-3] = to_z(got[2], 1), to_z(got[-2], -1)
    return [got[k] for k in SHIFTS]


def step(density, pattern):
    piece, block = shape(BLK, BLK, bf16), shape(1024, BLK, bf16)
    raw = cross(density)
    own = [pltpu.SMEM((32, 32), jnp.int32), pltpu.VMEM((1024, BLK), bf16), pltpu.SemaphoreType.DMA((2,))]
    outs = [block, shape(64, BLK, jnp.int32)] + [piece] * 4
    sparse, flags, *pieces = call(mask_kernel, outs, [HBM] * 2, scratch=own, params=WIDE)(pattern, density)
    pieces = [pieces[0]] + [to_x(pieces[k], k) for k in (1, 2, 3)]
    shard = call(shard_kernel, shape(BLK, 512, bf16), [VMEM] * 4)(*pieces)
    lefts = gather_z(shard)

    blocks = [sparse] + [to_x(sparse, k) for k in (1, 2, 3)]
    mine = call(half_kernel, shape(1024, 512, bf16), [VMEM] * 4)(*blocks)
    theirs = to_core(mine)
    crossed = call(mask_crossed_kernel, block, [VMEM] * 2)(flags, raw)
    far = cross(blocks[2])
    blocks = [crossed, to_x(crossed, 1), far, to_x(crossed, 3)]
    blocks = blocks + [to_core(b) for b in blocks]
    panel = call(panel_kernel, shape(4096, 512, bf16), [VMEM] * 10, nbytes=8 << 20)(mine, theirs, *blocks)

    flops = 2 * 128 * 4096 * 512
    square, half = call(square_kernel, [shape(BLK, 512, f32), shape(BLK, 512, bf16)], [VMEM] * 9, flops, 5 << 20)(*lefts, panel)
    lefts = gather_z_apart(half)
    early = call(early_kernel, shape(BLK, 512, f32), [VMEM] * 6, flops, 5 << 20)(*lefts[:5], panel)
    pieces = call(cube_kernel, [shape(BLK, BLK, f32)] * 4, [VMEM] * 6, flops, 5 << 20, [pltpu.VMEM((BLK, 512), f32)])(*lefts[5:], panel, square, early)
    pieces = [pieces[0]] + [to_x(pieces[k], k) for k in (1, 2, 3)]
    return call(join_kernel, shape(512, BLK, f32), [VMEM] * 4)(*pieces)


def solution(mesh):
    fine = Mesh(mesh.devices.reshape(2, 2, NZ, NX, 2), AXES)
    return jax.shard_map(
        step,
        mesh=fine,
        in_specs=(P(("yh", "core"), ("z", "x")), P()),
        out_specs=P(("yh", "core", "yl"), ("z", "x")),
        check_vma=False,
    )
```

```python
import jax
import jax.numpy as jnp
from jax import lax
from jax.experimental import pallas as pl
from jax.experimental.pallas import tpu as pltpu
from jax.sharding import Mesh, PartitionSpec as P


AXES = ("yh", "core", "z", "x", "yl")
NX, NZ = 4, 8
BLK = 128
VMEM = pl.BlockSpec(memory_space=pltpu.VMEM)
HBM = pl.BlockSpec(memory_space=pltpu.HBM)
bf16, f32 = jnp.bfloat16, jnp.float32
PARAMS = pltpu.CompilerParams(vmem_limit_bytes=16 << 20)


def call(kernel, outs, ins, flops=0, nbytes=0, scratch=()):
    return pl.pallas_call(
        kernel,
        out_shape=outs,
        in_specs=ins,
        out_specs=jax.tree.map(lambda _: VMEM, outs),
        scratch_shapes=scratch,
        compiler_params=PARAMS,
        cost_estimate=pl.CostEstimate(flops=flops, bytes_accessed=nbytes, transcendentals=0),
    )


def shape(rows, cols, dtype):
    return jax.ShapeDtypeStruct((rows, cols), dtype)


def to_x(a, k):
    return lax.ppermute(a, "x", [(i, (i + k) % NX) for i in range(NX)])


def along_z(a, k):
    pairs = [(z, (z + k) % NZ) for z in range(NZ)] + [(NZ + z, NZ + (z - k) % NZ) for z in range(NZ)]
    return lax.ppermute(a, ("core", "z"), pairs)


def to_z(a, k):
    return lax.ppermute(a, "z", [(z, (z + k) % NZ) for z in range(NZ)])


def to_core(a):
    return lax.ppermute(a, "core", [(0, 1), (1, 0)])


def cross(a):
    return lax.ppermute(a, ("yh", "yl"), [(0, 3), (3, 0), (1, 2), (2, 1)])


def at(i, size=BLK):
    return pl.ds(pl.multiple_of(i * size, size), size)


def back(i, k, n):
    return lax.rem(i - k + n, n)


def mask_kernel(pattern, density, sparse, crossed_flags, *rest):
    *pieces, flags, block, sems = rest
    copies = [
        pltpu.make_async_copy(pattern, flags, sems.at[0]),
        pltpu.make_async_copy(density, block, sems.at[1]),
    ]
    for copy in copies:
        copy.start()
    for copy in copies:
        copy.wait()
    yh, core = lax.axis_index("yh"), lax.axis_index("core")
    column = lax.axis_index("z") * NX + lax.axis_index("x")
    for i in range(8):
        rows = slice(i * BLK, (i + 1) * BLK)
        value = block[rows, :]
        sparse[rows, :] = jnp.where(flags[(yh * 2 + core) * 8 + i, column] == 1, value, jnp.zeros_like(value))
        flag = flags[((1 - yh) * 2 + core) * 8 + i, column]
        crossed_flags[i * 8 : i * 8 + 8, :] = jnp.broadcast_to(flag, (8, BLK)).astype(jnp.int32)
    x, yl = lax.axis_index("x"), lax.axis_index("yl")
    for k, piece in enumerate(pieces):
        piece[...] = sparse[at(yl * 4 + lax.rem(x + k, NX)), :]


def mask_crossed_kernel(flags, block, out):
    for i in range(8):
        rows = slice(i * BLK, (i + 1) * BLK)
        value = block[rows, :]
        keep = jnp.broadcast_to(flags[i * 8 : i * 8 + 1, :], (BLK, BLK)) == 1
        out[rows, :] = jnp.where(keep, value.astype(f32), 0.0).astype(bf16)


def shard_kernel(*refs):
    *pieces, shard = refs
    x = lax.axis_index("x")
    for k, piece in enumerate(pieces):
        shard[:, at(back(x, k, NX))] = piece[...]


def half_kernel(*refs):
    *blocks, half = refs
    x = lax.axis_index("x")
    for k, block in enumerate(blocks):
        half[:, at(back(x, k, NX))] = block[...]


def panel_kernel(*refs):
    mine, theirs, *blocks, panel = refs
    x, yh, core = lax.axis_index("x"), lax.axis_index("yh"), lax.axis_index("core")
    panel[at(yh * 2 + core, 1024), :] = mine[...]
    panel[at(yh * 2 + 1 - core, 1024), :] = theirs[...]
    for n, block in enumerate(blocks):
        k, dcore = n % 4, n // 4
        group = (1 - yh) * 2 + lax.rem(core + dcore, 2)
        panel[at(group, 1024), at(back(x, k, NX))] = block[...]


def first_panel_kernel(*refs):
    mine, theirs, *blocks, panel = refs
    x, yh, core = lax.axis_index("x"), lax.axis_index("yh"), lax.axis_index("core")
    panel[at(yh * 2 + core, 1024), :] = mine[...]
    panel[at(yh * 2 + 1 - core, 1024), :] = theirs[...]
    for n, block in enumerate(blocks):
        k, dcore = (0, 1, 3)[n % 3], n // 3
        group = (1 - yh) * 2 + lax.rem(core + dcore, 2)
        panel[at(group, 1024), at(back(x, k, NX))] = block[...]
    panel[at(1 - yh, 2048), at(lax.rem(x + 2, NX))] = jnp.zeros((2048, BLK), bf16)


def join_cores_kernel(mine, other, both):
    core = lax.axis_index("core")
    both[at(core), :] = mine[...]
    both[at(1 - core), :] = other[...]


def split_kernel(both, *parts):
    core = lax.axis_index("core")
    parts[0][...] = both[at(1 - core), :]
    if len(parts) > 1:
        parts[1][...] = both[at(core), :]


def term(lhs, k, panel):
    owner = lax.rem(lax.axis_index("z") - k + NZ, NZ)
    return jnp.dot(lhs, panel[at(owner, 512), :], preferred_element_type=f32)


def first_square_kernel(own, near2, near1, near3, back2, back1, back3, panel, total, row):
    core, z = lax.axis_index("core"), lax.axis_index("z")
    sign = 1 - 2 * core
    parts = [(0, own[...])]
    parts += [(k, ref[at(core), :]) for k, ref in ((1, near1), (2, near2), (3, near3))]
    parts += [(k, ref[...]) for k, ref in ((-1, back1), (-2, back2), (-3, back3))]
    value = None
    for k, part in parts:
        owner = lax.rem(z - sign * k + NZ, NZ)
        row[:, at(owner, 512)] = part
        product = jnp.dot(part, panel[at(owner, 512), :], preferred_element_type=f32)
        value = product if value is None else value + product
    row[:, at(lax.rem(z + 4, NZ), 512)] = jnp.zeros((BLK, 512), bf16)
    total[...] = value


def last_square_kernel(total, row, far_shard, panel, far, other, square, half, column):
    x, z = lax.axis_index("x"), lax.axis_index("z")
    yh, core = lax.axis_index("yh"), lax.axis_index("core")
    owner = lax.rem(z + 4, NZ)
    column[at(core, 1024), :] = far[...]
    column[at(1 - core, 1024), :] = other[...]
    shard = far_shard[...]
    square[...] = total[...] + jnp.dot(shard, panel[at(owner, 512), :], preferred_element_type=f32)
    inside = jnp.where(owner // 4 == 1 - yh, shard, jnp.zeros_like(shard))
    extra = jnp.dot(row[:, at(1 - yh, 2048)], column[...], preferred_element_type=f32)
    extra += jnp.dot(inside, column[at(lax.rem(owner, 4), 512), :], preferred_element_type=f32)
    square[:, at(lax.rem(x + 2, NX))] += extra
    half[...] = square[...].astype(bf16)


SHIFTS = (0, 1, -1, 2, -2, 3, -3, 4)


def early_kernel(*refs):
    *lefts, panel, cube = refs
    total = None
    for k, ref in zip(SHIFTS, lefts):
        part = term(ref[...], k, panel)
        total = part if total is None else total + part
    cube[...] = total


def cube_kernel(*refs):
    lefts, (panel, square, cube), pieces, total = refs[:3], refs[3:6], refs[6:10], refs[10]
    late = cube[...]
    for k, ref in zip(SHIFTS[5:], lefts):
        late += term(ref[...], k, panel)
    total[...] = 3.0 * square[...] - 2.0 * late
    x = lax.axis_index("x")
    for k, piece in enumerate(pieces):
        piece[...] = total[:, at(lax.rem(x + k, NX))]


def pick_kernel(first, second, out):
    out[...] = jnp.where(lax.axis_index("core") == 0, first[...], second[...])


def join_kernel(*refs):
    *pieces, out = refs
    x = lax.axis_index("x")
    for k, piece in enumerate(pieces):
        out[at(back(x, k, NX)), :] = piece[...]


def gather_z(own):
    part = shape(BLK, 512, bf16)
    other = to_core(own)
    both = call(join_cores_kernel, shape(2 * BLK, 512, bf16), [VMEM] * 2)(own, other)
    near2 = along_z(both, 2)
    near1 = along_z(both, 1)
    near3 = along_z(near2, 1)
    send2, relay = call(split_kernel, [part] * 2, [VMEM])(near2)
    far = along_z(relay, 2)
    back2 = to_core(send2)
    back1 = to_core(call(split_kernel, [part], [VMEM])(near1)[0])
    back3 = to_core(call(split_kernel, [part], [VMEM])(near3)[0])
    return [own, near2, near1, near3, far, back2, back1, back3]


def gather_z_apart(own):
    got = {0: own}
    for k in (2, -2, 1, -1):
        got[k] = to_z(own, k)
    got[4] = along_z(call(pick_kernel, shape(BLK, 512, bf16), [VMEM] * 2)(got[2], got[-2]), 2)
    got[3], got[-3] = to_z(got[2], 1), to_z(got[-2], -1)
    return [got[k] for k in SHIFTS]


def step(density, pattern):
    piece, block = shape(BLK, BLK, bf16), shape(1024, BLK, bf16)
    raw = cross(density)
    own = [pltpu.SMEM((32, 32), jnp.int32), pltpu.VMEM((1024, BLK), bf16), pltpu.SemaphoreType.DMA((2,))]
    outs = [block, shape(64, BLK, jnp.int32)] + [piece] * 4
    sparse, flags, *pieces = call(mask_kernel, outs, [HBM] * 2, scratch=own)(*(pltpu.with_memory_space_constraint(a, pltpu.HBM) for a in (pattern, density)))
    pieces = [pieces[0]] + [to_x(pieces[k], k) for k in (1, 2, 3)]
    shard = call(shard_kernel, shape(BLK, 512, bf16), [VMEM] * 4)(*pieces)
    lefts = gather_z(shard)

    blocks = [sparse] + [to_x(sparse, k) for k in (1, 2, 3)]
    mine = call(half_kernel, shape(1024, 512, bf16), [VMEM] * 4)(*blocks)
    theirs = to_core(mine)
    crossed = call(mask_crossed_kernel, block, [VMEM] * 2)(flags, raw)
    far = cross(blocks[2])
    blocks = [crossed, to_x(crossed, 1), far, to_x(crossed, 3)]
    blocks = blocks + [to_core(b) for b in blocks]
    flops = 2 * 128 * 4096 * 512
    first = call(first_panel_kernel, shape(4096, 512, bf16), [VMEM] * 8)(mine, theirs, *(blocks[n] for n in (0, 1, 3, 4, 5, 7)))
    total, row = call(first_square_kernel, [shape(BLK, 512, f32), shape(BLK, 4096, bf16)], [VMEM] * 8, flops, 5 << 20)(*lefts[:4], *lefts[5:], first)
    square, half = call(
        last_square_kernel, [shape(BLK, 512, f32), shape(BLK, 512, bf16)], [VMEM] * 6, flops // 8, 1 << 20, [pltpu.VMEM((2048, BLK), bf16)]
    )(total, row, lefts[4], first, blocks[2], blocks[6])
    panel = call(panel_kernel, shape(4096, 512, bf16), [VMEM] * 10, nbytes=8 << 20)(mine, theirs, *blocks)
    lefts = gather_z_apart(half)
    early = call(early_kernel, shape(BLK, 512, f32), [VMEM] * 6, flops, 5 << 20)(*lefts[:5], panel)
    pieces = call(cube_kernel, [shape(BLK, BLK, f32)] * 4, [VMEM] * 6, flops, 5 << 20, [pltpu.VMEM((BLK, 512), f32)])(*lefts[5:], panel, square, early)
    pieces = [pieces[0]] + [to_x(pieces[k], k) for k in (1, 2, 3)]
    return call(join_kernel, shape(512, BLK, f32), [VMEM] * 4)(*pieces)


def solution(mesh):
    fine = Mesh(mesh.devices.reshape(2, 2, NZ, NX, 2), AXES)
    return jax.shard_map(
        step,
        mesh=fine,
        in_specs=(P(("yh", "core"), ("z", "x")), P()),
        out_specs=P(("yh", "core", "yl"), ("z", "x")),
        check_vma=False,
    )
```

```python
import jax
import jax.numpy as jnp
from jax import lax
from jax.experimental import pallas as pl
from jax.experimental.pallas import tpu as pltpu
from jax.sharding import Mesh, PartitionSpec as P


AXES = ("yh", "core", "z", "x", "yl")
NX, NZ = 4, 8
BLK = 128
VMEM = pl.BlockSpec(memory_space=pltpu.VMEM)
HBM = pl.BlockSpec(memory_space=pltpu.HBM)
bf16, f32 = jnp.bfloat16, jnp.float32
PARAMS = pltpu.CompilerParams(vmem_limit_bytes=16 << 20)


def call(kernel, outs, ins, flops=0, nbytes=0, scratch=()):
    return pl.pallas_call(
        kernel,
        out_shape=outs,
        in_specs=ins,
        out_specs=jax.tree.map(lambda _: VMEM, outs),
        scratch_shapes=scratch,
        compiler_params=PARAMS,
        cost_estimate=pl.CostEstimate(flops=flops, bytes_accessed=nbytes, transcendentals=0),
    )


def shape(rows, cols, dtype):
    return jax.ShapeDtypeStruct((rows, cols), dtype)


def to_x(a, k):
    return lax.ppermute(a, "x", [(i, (i + k) % NX) for i in range(NX)])


def along_z(a, k):
    pairs = [(z, (z + k) % NZ) for z in range(NZ)] + [(NZ + z, NZ + (z - k) % NZ) for z in range(NZ)]
    return lax.ppermute(a, ("core", "z"), pairs)


def to_z(a, k):
    return lax.ppermute(a, "z", [(z, (z + k) % NZ) for z in range(NZ)])


def to_core(a):
    return lax.ppermute(a, "core", [(0, 1), (1, 0)])


def cross(a):
    return lax.ppermute(a, ("yh", "yl"), [(0, 3), (3, 0), (1, 2), (2, 1)])


def at(i, size=BLK):
    return pl.ds(pl.multiple_of(i * size, size), size)


def back(i, k, n):
    return lax.rem(i - k + n, n)


def mask_kernel(pattern, density, sparse, *rest):
    *pieces, flags, block, sems = rest
    copies = [
        pltpu.make_async_copy(pattern, flags, sems.at[0]),
        pltpu.make_async_copy(density, block, sems.at[1]),
    ]
    for copy in copies:
        copy.start()
    for copy in copies:
        copy.wait()
    yh, core = lax.axis_index("yh"), lax.axis_index("core")
    column = lax.axis_index("z") * NX + lax.axis_index("x")
    for i in range(8):
        rows = slice(i * BLK, (i + 1) * BLK)
        value = block[rows, :]
        sparse[rows, :] = jnp.where(flags[(yh * 2 + core) * 8 + i, column] == 1, value, jnp.zeros_like(value))
    x, yl = lax.axis_index("x"), lax.axis_index("yl")
    for k, piece in enumerate(pieces):
        piece[...] = sparse[at(yl * 4 + lax.rem(x + k, NX)), :]


def shard_kernel(*refs):
    *pieces, shard = refs
    x = lax.axis_index("x")
    for k, piece in enumerate(pieces):
        shard[:, at(back(x, k, NX))] = piece[...]


def half_kernel(*refs):
    *blocks, half = refs
    x = lax.axis_index("x")
    for k, block in enumerate(blocks):
        half[:, at(back(x, k, NX))] = block[...]


def panel_kernel(*refs):
    mine, theirs, *blocks, panel = refs
    x, yh, core = lax.axis_index("x"), lax.axis_index("yh"), lax.axis_index("core")
    panel[at(yh * 2 + core, 1024), :] = mine[...]
    panel[at(yh * 2 + 1 - core, 1024), :] = theirs[...]
    for n, block in enumerate(blocks):
        k, dcore = n % 4, n // 4
        group = (1 - yh) * 2 + lax.rem(core + dcore, 2)
        panel[at(group, 1024), at(back(x, k, NX))] = block[...]


def first_panel_kernel(*refs):
    mine, theirs, *blocks, panel = refs
    x, yh, core = lax.axis_index("x"), lax.axis_index("yh"), lax.axis_index("core")
    panel[at(yh * 2 + core, 1024), :] = mine[...]
    panel[at(yh * 2 + 1 - core, 1024), :] = theirs[...]
    for n, block in enumerate(blocks):
        k, dcore = (0, 1, 3)[n % 3], n // 3
        group = (1 - yh) * 2 + lax.rem(core + dcore, 2)
        panel[at(group, 1024), at(back(x, k, NX))] = block[...]
    panel[at(1 - yh, 2048), at(lax.rem(x + 2, NX))] = jnp.zeros((2048, BLK), bf16)


def join_cores_kernel(mine, other, both):
    core = lax.axis_index("core")
    both[at(core), :] = mine[...]
    both[at(1 - core), :] = other[...]


def split_kernel(both, *parts):
    core = lax.axis_index("core")
    parts[0][...] = both[at(1 - core), :]
    if len(parts) > 1:
        parts[1][...] = both[at(core), :]


def term(lhs, k, panel):
    owner = lax.rem(lax.axis_index("z") - k + NZ, NZ)
    return jnp.dot(lhs, panel[at(owner, 512), :], preferred_element_type=f32)


def first_square_kernel(own, near2, near1, near3, back2, back1, back3, panel, total, row):
    core, z = lax.axis_index("core"), lax.axis_index("z")
    sign = 1 - 2 * core
    parts = [(0, own[...])]
    parts += [(k, ref[at(core), :]) for k, ref in ((1, near1), (2, near2), (3, near3))]
    parts += [(k, ref[...]) for k, ref in ((-1, back1), (-2, back2), (-3, back3))]
    value = None
    for k, part in parts:
        owner = lax.rem(z - sign * k + NZ, NZ)
        row[:, at(owner, 512)] = part
        product = jnp.dot(part, panel[at(owner, 512), :], preferred_element_type=f32)
        value = product if value is None else value + product
    row[:, at(lax.rem(z + 4, NZ), 512)] = jnp.zeros((BLK, 512), bf16)
    total[...] = value


def last_square_kernel(total, row, far_shard, panel, far, other, square, half, column):
    x, z = lax.axis_index("x"), lax.axis_index("z")
    yh, core = lax.axis_index("yh"), lax.axis_index("core")
    owner = lax.rem(z + 4, NZ)
    column[at(core, 1024), :] = far[...]
    column[at(1 - core, 1024), :] = other[...]
    shard = far_shard[...]
    square[...] = total[...] + jnp.dot(shard, panel[at(owner, 512), :], preferred_element_type=f32)
    inside = jnp.where(owner // 4 == 1 - yh, shard, jnp.zeros_like(shard))
    extra = jnp.dot(row[:, at(1 - yh, 2048)], column[...], preferred_element_type=f32)
    extra += jnp.dot(inside, column[at(lax.rem(owner, 4), 512), :], preferred_element_type=f32)
    square[:, at(lax.rem(x + 2, NX))] += extra
    half[...] = square[...].astype(bf16)


SHIFTS = (0, 1, -1, 2, -2, 3, -3, 4)


def early_kernel(*refs):
    *lefts, panel, cube = refs
    total = None
    for k, ref in zip(SHIFTS, lefts):
        part = term(ref[...], k, panel)
        total = part if total is None else total + part
    cube[...] = total


def cube_kernel(*refs):
    lefts, (panel, square, cube), pieces, total = refs[:3], refs[3:6], refs[6:10], refs[10]
    late = cube[...]
    for k, ref in zip(SHIFTS[5:], lefts):
        late += term(ref[...], k, panel)
    total[...] = 3.0 * square[...] - 2.0 * late
    x = lax.axis_index("x")
    for k, piece in enumerate(pieces):
        piece[...] = total[:, at(lax.rem(x + k, NX))]


def pick_kernel(first, second, out):
    out[...] = jnp.where(lax.axis_index("core") == 0, first[...], second[...])


def join_kernel(*refs):
    *pieces, out, sems = refs
    x = lax.axis_index("x")
    copies = [
        pltpu.make_async_copy(piece, out.at[at(back(x, k, NX)), :], sems.at[k]) for k, piece in enumerate(pieces)
    ]
    for copy in copies:
        copy.start()
    for copy in copies:
        copy.wait()


def gather_z(own):
    part = shape(BLK, 512, bf16)
    other = to_core(own)
    both = call(join_cores_kernel, shape(2 * BLK, 512, bf16), [VMEM] * 2)(own, other)
    near2 = along_z(both, 2)
    near1 = along_z(both, 1)
    near3 = along_z(near2, 1)
    send2, relay = call(split_kernel, [part] * 2, [VMEM])(near2)
    far = along_z(relay, 2)
    back2 = to_core(send2)
    back1 = to_core(call(split_kernel, [part], [VMEM])(near1)[0])
    back3 = to_core(call(split_kernel, [part], [VMEM])(near3)[0])
    return [own, near2, near1, near3, far, back2, back1, back3]


def gather_z_apart(own):
    got = {0: own}
    for k in (2, -2, 1, -1):
        got[k] = to_z(own, k)
    got[4] = along_z(call(pick_kernel, shape(BLK, 512, bf16), [VMEM] * 2)(got[2], got[-2]), 2)
    got[3], got[-3] = to_z(got[2], 1), to_z(got[-2], -1)
    return [got[k] for k in SHIFTS]


def step(density, pattern):
    piece, block = shape(BLK, BLK, bf16), shape(1024, BLK, bf16)
    own = [pltpu.SMEM((32, 32), jnp.int32), pltpu.VMEM((1024, BLK), bf16), pltpu.SemaphoreType.DMA((2,))]
    outs = [block] + [piece] * 4
    sparse, *pieces = call(mask_kernel, outs, [HBM] * 2, scratch=own)(*(pltpu.with_memory_space_constraint(a, pltpu.HBM) for a in (pattern, density)))
    pieces = [pieces[0]] + [to_x(pieces[k], k) for k in (1, 2, 3)]
    shard = call(shard_kernel, shape(BLK, 512, bf16), [VMEM] * 4)(*pieces)
    lefts = gather_z(shard)

    blocks = [sparse] + [to_x(sparse, k) for k in (1, 2, 3)]
    mine = call(half_kernel, shape(1024, 512, bf16), [VMEM] * 4)(*blocks)
    theirs = to_core(mine)
    crossed = cross(sparse)
    far = cross(blocks[2])
    blocks = [crossed, to_x(crossed, 1), far, to_x(crossed, 3)]
    blocks = blocks + [to_core(b) for b in blocks]
    flops = 2 * 128 * 4096 * 512
    first = call(first_panel_kernel, shape(4096, 512, bf16), [VMEM] * 8)(mine, theirs, *(blocks[n] for n in (0, 1, 3, 4, 5, 7)))
    total, row = call(first_square_kernel, [shape(BLK, 512, f32), shape(BLK, 4096, bf16)], [VMEM] * 8, flops, 5 << 20)(*lefts[:4], *lefts[5:], first)
    square, half = call(
        last_square_kernel, [shape(BLK, 512, f32), shape(BLK, 512, bf16)], [VMEM] * 6, flops // 8, 1 << 20, [pltpu.VMEM((2048, BLK), bf16)]
    )(total, row, lefts[4], first, blocks[2], blocks[6])
    panel = call(panel_kernel, shape(4096, 512, bf16), [VMEM] * 10, nbytes=8 << 20)(mine, theirs, *blocks)
    lefts = gather_z_apart(half)
    early = call(early_kernel, shape(BLK, 512, f32), [VMEM] * 6, flops, 5 << 20)(*lefts[:5], panel)
    pieces = call(cube_kernel, [shape(BLK, BLK, f32)] * 4, [VMEM] * 6, flops, 5 << 20, [pltpu.VMEM((BLK, 512), f32)])(*lefts[5:], panel, square, early)
    pieces = [pieces[0]] + [to_x(pieces[k], k) for k in (1, 2, 3)]
    return pl.pallas_call(
        join_kernel,
        out_shape=shape(512, BLK, f32),
        in_specs=[VMEM] * 4,
        out_specs=HBM,
        scratch_shapes=[pltpu.SemaphoreType.DMA((4,))],
        compiler_params=PARAMS,
    )(*pieces)


def solution(mesh):
    fine = Mesh(mesh.devices.reshape(2, 2, NZ, NX, 2), AXES)
    return jax.shard_map(
        step,
        mesh=fine,
        in_specs=(P(("yh", "core"), ("z", "x")), P()),
        out_specs=P(("yh", "core", "yl"), ("z", "x")),
        check_vma=False,
    )
```

```python
import jax
import jax.numpy as jnp
from jax import lax
from jax.experimental import pallas as pl
from jax.experimental.pallas import tpu as pltpu
from jax.sharding import Mesh, PartitionSpec as P


AXES = ("yh", "core", "z", "x", "yl")
NX, NZ = 4, 8
BLK = 128
VMEM = pl.BlockSpec(memory_space=pltpu.VMEM)
HBM = pl.BlockSpec(memory_space=pltpu.HBM)
bf16, f32 = jnp.bfloat16, jnp.float32
PARAMS = pltpu.CompilerParams(vmem_limit_bytes=16 << 20)


def call(kernel, outs, ins, flops=0, nbytes=0, scratch=()):
    return pl.pallas_call(
        kernel,
        out_shape=outs,
        in_specs=ins,
        out_specs=jax.tree.map(lambda _: VMEM, outs),
        scratch_shapes=scratch,
        compiler_params=PARAMS,
        cost_estimate=pl.CostEstimate(flops=flops, bytes_accessed=nbytes, transcendentals=0),
    )


def shape(rows, cols, dtype):
    return jax.ShapeDtypeStruct((rows, cols), dtype)


def to_x(a, k):
    return lax.ppermute(a, "x", [(i, (i + k) % NX) for i in range(NX)])


def along_z(a, k):
    pairs = [(z, (z + k) % NZ) for z in range(NZ)] + [(NZ + z, NZ + (z - k) % NZ) for z in range(NZ)]
    return lax.ppermute(a, ("core", "z"), pairs)


def to_z(a, k):
    return lax.ppermute(a, "z", [(z, (z + k) % NZ) for z in range(NZ)])


def to_core(a):
    return lax.ppermute(a, "core", [(0, 1), (1, 0)])


def cross(a):
    return lax.ppermute(a, ("yh", "yl"), [(0, 3), (3, 0), (1, 2), (2, 1)])


def at(i, size=BLK):
    return pl.ds(pl.multiple_of(i * size, size), size)


def back(i, k, n):
    return lax.rem(i - k + n, n)


def mask_kernel(pattern, density, sparse, *rest):
    *pieces, flags, block, sems = rest
    copies = [
        pltpu.make_async_copy(pattern, flags, sems.at[0]),
        pltpu.make_async_copy(density, block, sems.at[1]),
    ]
    for copy in copies:
        copy.start()
    for copy in copies:
        copy.wait()
    yh, core = lax.axis_index("yh"), lax.axis_index("core")
    column = lax.axis_index("z") * NX + lax.axis_index("x")
    for i in range(8):
        rows = slice(i * BLK, (i + 1) * BLK)
        value = block[rows, :]
        sparse[rows, :] = jnp.where(flags[(yh * 2 + core) * 8 + i, column] == 1, value, jnp.zeros_like(value))
    x, yl = lax.axis_index("x"), lax.axis_index("yl")
    for k, piece in enumerate(pieces):
        piece[...] = sparse[at(yl * 4 + lax.rem(x + k, NX)), :]


def shard_kernel(*refs):
    *pieces, shard = refs
    x = lax.axis_index("x")
    for k, piece in enumerate(pieces):
        shard[:, at(back(x, k, NX))] = piece[...]


def half_kernel(*refs):
    *blocks, half = refs
    x = lax.axis_index("x")
    for k, block in enumerate(blocks):
        half[:, at(back(x, k, NX))] = block[...]


def rest_kernel(own, near, away, rest):
    x = lax.axis_index("x")
    for k, block in ((0, own), (1, near), (3, away)):
        rest[:, at(back(x, k, NX))] = block[...]
    rest[:, at(lax.rem(x + 2, NX))] = jnp.zeros((1024, BLK), bf16)


def first_panel_kernel(mine, theirs, rest, other, panel):
    yh, core = lax.axis_index("yh"), lax.axis_index("core")
    panel[at(yh * 2 + core, 1024), :] = mine[...]
    panel[at(yh * 2 + 1 - core, 1024), :] = theirs[...]
    panel[at((1 - yh) * 2 + core, 1024), :] = rest[...]
    panel[at((1 - yh) * 2 + 1 - core, 1024), :] = other[...]


def panel_kernel(first, far, other, panel):
    x, yh, core = lax.axis_index("x"), lax.axis_index("yh"), lax.axis_index("core")
    panel[...] = first[...]
    opposite = at(lax.rem(x + 2, NX))
    panel[at((1 - yh) * 2 + core, 1024), opposite] = far[...]
    panel[at((1 - yh) * 2 + 1 - core, 1024), opposite] = other[...]


def join_cores_kernel(mine, other, both):
    core = lax.axis_index("core")
    both[at(core), :] = mine[...]
    both[at(1 - core), :] = other[...]


def split_kernel(both, *parts):
    core = lax.axis_index("core")
    parts[0][...] = both[at(1 - core), :]
    if len(parts) > 1:
        parts[1][...] = both[at(core), :]


def term(lhs, k, panel):
    owner = lax.rem(lax.axis_index("z") - k + NZ, NZ)
    return jnp.dot(lhs, panel[at(owner, 512), :], preferred_element_type=f32)


def first_square_kernel(own, near2, near1, near3, back2, back1, back3, panel, total, row):
    core, z = lax.axis_index("core"), lax.axis_index("z")
    sign = 1 - 2 * core
    parts = [(0, own[...])]
    parts += [(k, ref[at(core), :]) for k, ref in ((1, near1), (2, near2), (3, near3))]
    parts += [(k, ref[...]) for k, ref in ((-1, back1), (-2, back2), (-3, back3))]
    value = None
    for k, part in parts:
        owner = lax.rem(z - sign * k + NZ, NZ)
        row[:, at(owner, 512)] = part
        product = jnp.dot(part, panel[at(owner, 512), :], preferred_element_type=f32)
        value = product if value is None else value + product
    row[:, at(lax.rem(z + 4, NZ), 512)] = jnp.zeros((BLK, 512), bf16)
    total[...] = value


def last_square_kernel(total, row, far_shard, panel, far, other, square, half, column):
    x, z = lax.axis_index("x"), lax.axis_index("z")
    yh, core = lax.axis_index("yh"), lax.axis_index("core")
    owner = lax.rem(z + 4, NZ)
    column[at(core, 1024), :] = far[...]
    column[at(1 - core, 1024), :] = other[...]
    shard = far_shard[...]
    square[...] = total[...] + jnp.dot(shard, panel[at(owner, 512), :], preferred_element_type=f32)
    inside = jnp.where(owner // 4 == 1 - yh, shard, jnp.zeros_like(shard))
    extra = jnp.dot(row[:, at(1 - yh, 2048)], column[...], preferred_element_type=f32)
    extra += jnp.dot(inside, column[at(lax.rem(owner, 4), 512), :], preferred_element_type=f32)
    square[:, at(lax.rem(x + 2, NX))] += extra
    half[...] = square[...].astype(bf16)


SHIFTS = (0, 1, -1, 2, -2, 3, -3, 4)


def early_kernel(*refs):
    *lefts, panel, cube = refs
    total = None
    for k, ref in zip(SHIFTS, lefts):
        part = term(ref[...], k, panel)
        total = part if total is None else total + part
    cube[...] = total


def cube_kernel(*refs):
    lefts, (panel, square, cube), pieces, total = refs[:3], refs[3:6], refs[6:10], refs[10]
    late = cube[...]
    for k, ref in zip(SHIFTS[5:], lefts):
        late += term(ref[...], k, panel)
    total[...] = 3.0 * square[...] - 2.0 * late
    x = lax.axis_index("x")
    for k, piece in enumerate(pieces):
        piece[...] = total[:, at(lax.rem(x + k, NX))]


def pick_kernel(first, second, out):
    out[...] = jnp.where(lax.axis_index("core") == 0, first[...], second[...])


def join_kernel(*refs):
    *pieces, out = refs
    x = lax.axis_index("x")
    for k, piece in enumerate(pieces):
        out[at(back(x, k, NX)), :] = piece[...]


def gather_z(own):
    part = shape(BLK, 512, bf16)
    other = to_core(own)
    both = call(join_cores_kernel, shape(2 * BLK, 512, bf16), [VMEM] * 2)(own, other)
    near2 = along_z(both, 2)
    near1 = along_z(both, 1)
    near3 = along_z(near2, 1)
    send2, relay = call(split_kernel, [part] * 2, [VMEM])(near2)
    far = along_z(relay, 2)
    back2 = to_core(send2)
    back1 = to_core(call(split_kernel, [part], [VMEM])(near1)[0])
    back3 = to_core(call(split_kernel, [part], [VMEM])(near3)[0])
    return [own, near2, near1, near3, far, back2, back1, back3]


def gather_z_apart(own):
    got = {0: own}
    for k in (2, -2, 1, -1):
        got[k] = to_z(own, k)
    got[4] = along_z(call(pick_kernel, shape(BLK, 512, bf16), [VMEM] * 2)(got[2], got[-2]), 2)
    got[3], got[-3] = to_z(got[2], 1), to_z(got[-2], -1)
    return [got[k] for k in SHIFTS]


def step(density, pattern):
    piece, block = shape(BLK, BLK, bf16), shape(1024, BLK, bf16)
    own = [pltpu.SMEM((32, 32), jnp.int32), pltpu.VMEM((1024, BLK), bf16), pltpu.SemaphoreType.DMA((2,))]
    outs = [block] + [piece] * 4
    sparse, *pieces = call(mask_kernel, outs, [HBM] * 2, scratch=own)(*(pltpu.with_memory_space_constraint(a, pltpu.HBM) for a in (pattern, density)))
    pieces = [pieces[0]] + [to_x(pieces[k], k) for k in (1, 2, 3)]
    shard = call(shard_kernel, shape(BLK, 512, bf16), [VMEM] * 4)(*pieces)
    lefts = gather_z(shard)

    blocks = [sparse] + [to_x(sparse, k) for k in (1, 2, 3)]
    mine = call(half_kernel, shape(1024, 512, bf16), [VMEM] * 4)(*blocks)
    theirs = to_core(mine)
    crossed = cross(sparse)
    far = cross(blocks[2])
    near, away = to_x(crossed, 1), to_x(crossed, 3)
    rest = call(rest_kernel, shape(1024, 512, bf16), [VMEM] * 3)(crossed, near, away)
    rest = [rest, to_core(rest)]
    far = [far, to_core(far)]

    flops = 2 * 128 * 4096 * 512
    first = call(first_panel_kernel, shape(4096, 512, bf16), [VMEM] * 4)(mine, theirs, *rest)
    total, row = call(first_square_kernel, [shape(BLK, 512, f32), shape(BLK, 4096, bf16)], [VMEM] * 8, flops, 5 << 20)(*lefts[:4], *lefts[5:], first)
    square, half = call(
        last_square_kernel, [shape(BLK, 512, f32), shape(BLK, 512, bf16)], [VMEM] * 6, flops // 8, 1 << 20, [pltpu.VMEM((2048, BLK), bf16)]
    )(total, row, lefts[4], first, *far)
    panel = call(panel_kernel, shape(4096, 512, bf16), [VMEM] * 3, nbytes=8 << 20)(first, *far)
    lefts = gather_z_apart(half)
    early = call(early_kernel, shape(BLK, 512, f32), [VMEM] * 6, flops, 5 << 20)(*lefts[:5], panel)
    pieces = call(cube_kernel, [shape(BLK, BLK, f32)] * 4, [VMEM] * 6, flops, 5 << 20, [pltpu.VMEM((BLK, 512), f32)])(*lefts[5:], panel, square, early)
    pieces = [pieces[0]] + [to_x(pieces[k], k) for k in (1, 2, 3)]
    return call(join_kernel, shape(512, BLK, f32), [VMEM] * 4)(*pieces)


def solution(mesh):
    fine = Mesh(mesh.devices.reshape(2, 2, NZ, NX, 2), AXES)
    return jax.shard_map(
        step,
        mesh=fine,
        in_specs=(P(("yh", "core"), ("z", "x")), P()),
        out_specs=P(("yh", "core", "yl"), ("z", "x")),
        check_vma=False,
    )
```

```python
import jax
import jax.numpy as jnp
from jax import lax
from jax.experimental import pallas as pl
from jax.experimental.pallas import tpu as pltpu
from jax.sharding import Mesh, PartitionSpec as P


AXES = ("yh", "core", "z", "x", "yl")
NX, NZ = 4, 8
BLK = 128
VMEM = pl.BlockSpec(memory_space=pltpu.VMEM)
HBM = pl.BlockSpec(memory_space=pltpu.HBM)
bf16, f32 = jnp.bfloat16, jnp.float32
PARAMS = pltpu.CompilerParams(vmem_limit_bytes=16 << 20)


def call(kernel, outs, ins, flops=0, nbytes=0, scratch=()):
    return pl.pallas_call(
        kernel,
        out_shape=outs,
        in_specs=ins,
        out_specs=jax.tree.map(lambda _: VMEM, outs),
        scratch_shapes=scratch,
        compiler_params=PARAMS,
        cost_estimate=pl.CostEstimate(flops=flops, bytes_accessed=nbytes, transcendentals=0),
    )


def shape(rows, cols, dtype):
    return jax.ShapeDtypeStruct((rows, cols), dtype)


def to_x(a, k):
    return lax.ppermute(a, "x", [(i, (i + k) % NX) for i in range(NX)])


def along_z(a, k):
    pairs = [(z, (z + k) % NZ) for z in range(NZ)] + [(NZ + z, NZ + (z - k) % NZ) for z in range(NZ)]
    return lax.ppermute(a, ("core", "z"), pairs)


def to_z(a, k):
    return lax.ppermute(a, "z", [(z, (z + k) % NZ) for z in range(NZ)])


def to_core(a):
    return lax.ppermute(a, "core", [(0, 1), (1, 0)])


def cross(a):
    return lax.ppermute(a, ("yh", "yl"), [(0, 3), (3, 0), (1, 2), (2, 1)])


def at(i, size=BLK):
    return pl.ds(pl.multiple_of(i * size, size), size)


def back(i, k, n):
    return lax.rem(i - k + n, n)


def mask_kernel(pattern, density, sparse, *rest):
    *pieces, flags, block, sems = rest
    copies = [
        pltpu.make_async_copy(pattern, flags, sems.at[0]),
        pltpu.make_async_copy(density, block, sems.at[1]),
    ]
    for copy in copies:
        copy.start()
    for copy in copies:
        copy.wait()
    yh, core = lax.axis_index("yh"), lax.axis_index("core")
    column = lax.axis_index("z") * NX + lax.axis_index("x")
    for i in range(8):
        rows = slice(i * BLK, (i + 1) * BLK)
        value = block[rows, :]
        sparse[rows, :] = jnp.where(flags[(yh * 2 + core) * 8 + i, column] == 1, value, jnp.zeros_like(value))
    x, yl = lax.axis_index("x"), lax.axis_index("yl")
    for k, piece in enumerate(pieces):
        piece[...] = sparse[at(yl * 4 + lax.rem(x + k, NX)), :]


def shard_kernel(*refs):
    *pieces, shard = refs
    x = lax.axis_index("x")
    for k, piece in enumerate(pieces):
        shard[:, at(back(x, k, NX))] = piece[...]


def half_kernel(*refs):
    *blocks, half = refs
    x = lax.axis_index("x")
    for k, block in enumerate(blocks):
        half[:, at(back(x, k, NX))] = block[...]


def panel_kernel(*refs):
    mine, theirs, *blocks, panel = refs
    x, yh, core = lax.axis_index("x"), lax.axis_index("yh"), lax.axis_index("core")
    panel[at(yh * 2 + core, 1024), :] = mine[...]
    panel[at(yh * 2 + 1 - core, 1024), :] = theirs[...]
    for n, block in enumerate(blocks):
        k, dcore = n % 4, n // 4
        group = (1 - yh) * 2 + lax.rem(core + dcore, 2)
        panel[at(group, 1024), at(back(x, k, NX))] = block[...]


def first_panel_kernel(*refs):
    mine, theirs, *blocks, panel = refs
    x, yh, core = lax.axis_index("x"), lax.axis_index("yh"), lax.axis_index("core")
    panel[at(yh * 2 + core, 1024), :] = mine[...]
    panel[at(yh * 2 + 1 - core, 1024), :] = theirs[...]
    for n, block in enumerate(blocks):
        k, dcore = (0, 1, 3)[n % 3], n // 3
        group = (1 - yh) * 2 + lax.rem(core + dcore, 2)
        panel[at(group, 1024), at(back(x, k, NX))] = block[...]
    panel[at(1 - yh, 2048), at(lax.rem(x + 2, NX))] = jnp.zeros((2048, BLK), bf16)


def join_cores_kernel(mine, other, both):
    core = lax.axis_index("core")
    both[at(core), :] = mine[...]
    both[at(1 - core), :] = other[...]


def split_kernel(both, *parts):
    core = lax.axis_index("core")
    parts[0][...] = both[at(1 - core), :]
    if len(parts) > 1:
        parts[1][...] = both[at(core), :]


def term(lhs, k, panel):
    owner = lax.rem(lax.axis_index("z") - k + NZ, NZ)
    return jnp.dot(lhs, panel[at(owner, 512), :], preferred_element_type=f32)


def first_square_kernel(own, near2, near1, near3, back2, back1, back3, panel, total, row):
    core, z = lax.axis_index("core"), lax.axis_index("z")
    sign = 1 - 2 * core
    parts = [(0, own[...])]
    parts += [(k, ref[at(core), :]) for k, ref in ((1, near1), (2, near2), (3, near3))]
    parts += [(k, ref[...]) for k, ref in ((-1, back1), (-2, back2), (-3, back3))]
    value = None
    for k, part in parts:
        owner = lax.rem(z - sign * k + NZ, NZ)
        row[:, at(owner, 512)] = part
        product = jnp.dot(part, panel[at(owner, 512), :], preferred_element_type=f32)
        value = product if value is None else value + product
    row[:, at(lax.rem(z + 4, NZ), 512)] = jnp.zeros((BLK, 512), bf16)
    total[...] = value


def last_square_kernel(total, row, far_shard, panel, far, other, square, half, column):
    x, z = lax.axis_index("x"), lax.axis_index("z")
    yh, core = lax.axis_index("yh"), lax.axis_index("core")
    owner = lax.rem(z + 4, NZ)
    column[at(core, 1024), :] = far[...]
    column[at(1 - core, 1024), :] = other[...]
    shard = far_shard[...]
    square[...] = total[...] + jnp.dot(shard, panel[at(owner, 512), :], preferred_element_type=f32)
    inside = jnp.where(owner // 4 == 1 - yh, shard, jnp.zeros_like(shard))
    extra = jnp.dot(row[:, at(1 - yh, 2048)], column[...], preferred_element_type=f32)
    extra += jnp.dot(inside, column[at(lax.rem(owner, 4), 512), :], preferred_element_type=f32)
    square[:, at(lax.rem(x + 2, NX))] += extra
    half[...] = square[...].astype(bf16)


SHIFTS = (0, 1, -1, 2, -2, 3, -3, 4)


def early_kernel(*refs):
    *lefts, panel, cube = refs
    total = None
    for k, ref in zip(SHIFTS, lefts):
        part = term(ref[...], k, panel)
        total = part if total is None else total + part
    cube[...] = total


def cube_kernel(*refs):
    lefts, (panel, square, cube), pieces, total = refs[:3], refs[3:6], refs[6:10], refs[10]
    late = cube[...]
    for k, ref in zip(SHIFTS[5:], lefts):
        late += term(ref[...], k, panel)
    total[...] = 3.0 * square[...] - 2.0 * late
    x = lax.axis_index("x")
    for k, piece in enumerate(pieces):
        piece[...] = total[:, at(lax.rem(x + k, NX))]


def pick_kernel(first, second, out):
    out[...] = jnp.where(lax.axis_index("core") == 0, first[...], second[...])


def join_kernel(*refs):
    *pieces, out = refs
    x = lax.axis_index("x")
    for k, piece in enumerate(pieces):
        out[at(back(x, k, NX)), :] = piece[...]


def gather_z(own):
    part = shape(BLK, 512, bf16)
    other = to_core(own)
    both = call(join_cores_kernel, shape(2 * BLK, 512, bf16), [VMEM] * 2)(own, other)
    near2 = along_z(both, 2)
    near1 = along_z(both, 1)
    near3 = along_z(near2, 1)
    send2, relay = call(split_kernel, [part] * 2, [VMEM])(near2)
    far = along_z(relay, 2)
    back2 = to_core(send2)
    back1 = to_core(call(split_kernel, [part], [VMEM])(near1)[0])
    back3 = to_core(call(split_kernel, [part], [VMEM])(near3)[0])
    return [own, near2, near1, near3, far, back2, back1, back3]


def gather_z_apart(own):
    got = {0: own}
    for k in (2, -2, 1, -1):
        got[k] = to_z(own, k)
    got[4] = along_z(call(pick_kernel, shape(BLK, 512, bf16), [VMEM] * 2)(got[2], got[-2]), 2)
    got[3], got[-3] = to_z(got[2], 1), to_z(got[-2], -1)
    return [got[k] for k in SHIFTS]


def step(density, pattern):
    piece, block = shape(BLK, BLK, bf16), shape(1024, BLK, bf16)
    own = [pltpu.SMEM((32, 32), jnp.int32), pltpu.VMEM((1024, BLK), bf16), pltpu.SemaphoreType.DMA((2,))]
    outs = [block] + [piece] * 4
    sparse, *pieces = call(mask_kernel, outs, [HBM] * 2, scratch=own)(*(pltpu.with_memory_space_constraint(a, pltpu.HBM) for a in (pattern, density)))
    pieces = [pieces[0]] + [to_x(pieces[k], k) for k in (1, 2, 3)]
    shard = call(shard_kernel, shape(BLK, 512, bf16), [VMEM] * 4)(*pieces)
    lefts = gather_z(shard)

    blocks = [sparse] + [to_x(sparse, k) for k in (1, 2, 3)]
    mine = call(half_kernel, shape(1024, 512, bf16), [VMEM] * 4)(*blocks)
    theirs = to_core(mine)
    crossed = cross(sparse)
    far = cross(blocks[2])
    blocks = [crossed, to_x(crossed, 1), far, to_x(crossed, 3)]
    blocks = blocks + [to_core(b) for b in blocks]
    flops = 2 * 128 * 4096 * 512
    first = call(first_panel_kernel, shape(4096, 512, bf16), [VMEM] * 8)(mine, theirs, *(blocks[n] for n in (0, 1, 3, 4, 5, 7)))
    total, row = call(first_square_kernel, [shape(BLK, 512, f32), shape(BLK, 4096, bf16)], [VMEM] * 8, flops, 5 << 20)(*lefts[:4], *lefts[5:], first)
    square, half = call(
        last_square_kernel, [shape(BLK, 512, f32), shape(BLK, 512, bf16)], [VMEM] * 6, flops // 8, 1 << 20, [pltpu.VMEM((2048, BLK), bf16)]
    )(total, row, lefts[4], first, blocks[2], blocks[6])
    panel = call(panel_kernel, shape(4096, 512, bf16), [VMEM] * 10, nbytes=8 << 20)(mine, theirs, *blocks)
    lefts = gather_z_apart(half)
    early = call(early_kernel, shape(BLK, 512, f32), [VMEM] * 6, flops, 5 << 20)(*lefts[:5], panel)
    pieces = call(cube_kernel, [shape(BLK, BLK, f32)] * 4, [VMEM] * 6, flops, 5 << 20, [pltpu.VMEM((BLK, 512), f32)])(*lefts[5:], panel, square, early)
    pieces = [pieces[0]] + [to_x(pieces[k], k) for k in (1, 2, 3)]
    return call(join_kernel, shape(512, BLK, f32), [VMEM] * 4)(*pieces)


def solution(mesh):
    fine = Mesh(mesh.devices.reshape(2, 2, NZ, NX, 2), AXES)
    return jax.shard_map(
        step,
        mesh=fine,
        in_specs=(P(("yh", "core"), ("z", "x")), P()),
        out_specs=P(("yh", "core", "yl"), ("z", "x")),
        check_vma=False,
    )
```
